1024 devices in a mesh: ctx: 64 (over y, z_hi, core), ch: 16 (over z_lo, x).
Axes of the slice: x: 4, y: 8, z: 16 (z_hi: 4, z_lo: 4; z = z_hi * 4 + z_lo), core: 2. Of those that a mesh axis runs over, the one named last changes fastest.
Arguments:
- q_mr: bfloat16 [1024, 32768], P('ch', 'ctx'), may hold values from -6 to 6
- k_mr: bfloat16 [1024, 32768], P('ch', 'ctx'), may hold values from -6 to 6
- v_mr: bfloat16 [1024, 32768], P('ch', 'ctx'), may hold values from -22 to 22
- mr_taps: bfloat16 [128, 1024], P(None, 'ch'), may hold values from -0.5 to 0.5
- norm_gain: float32 [1024], P('ch'), may hold values from 0.5 to 1.5
- q_li: bfloat16 [1024, 32768], P('ch', 'ctx'), may hold values from -6 to 6
- k_li: bfloat16 [1024, 32768], P('ch', 'ctx'), may hold values from -6 to 6
- rates: float32 [1024, 16], P('ch'), may hold values from 9.1552734e-06 to 0.0333333333, as said below
- residues: float32 [1024, 16], P('ch'), may hold values from -2 to 2
- skip: float32 [1024], P('ch'), may hold values from 0.5 to 1.5
Outputs:
- mixed: bfloat16 [1024, 32768], P('ch', 'ctx')
The draws below stay inside these ranges and needn't reach their ends.
Inputs may be any that keep to these rules, and one draw needn't show every extreme that they name: Positive decay rates.
All inputs are finite; a program needn't handle non-finite values.
Results may differ from the reference program's by a relative error of at most 0.0085.
Values may be sent and summed in bfloat16 or wider, within the bound.
A program may use at most 32 MiB of HBM per device.

```python
import math
import jax
import jax.numpy as jnp
from jax import lax

CH = 1024
TAPS = 128
MODES = 16
L = 32768


def draw_v_mr(key, part):
    first = jax.random.fold_in(jax.random.fold_in(key, 11), 0)
    base = jnp.clip(jax.random.normal(first, (CH, L), jnp.float32), -6.0, 6.0)
    scale = 0.6 * 3.0 ** (jnp.arange(CH, dtype=jnp.float32) / (CH - 1))
    return (base * scale[:, None]).astype(jnp.bfloat16)


def draw_rates(key, part):
    first, second, third = jax.random.split(jax.random.fold_in(key, 23), 3)
    share = 0.5
    fast = jax.random.uniform(first, (CH, MODES), jnp.float32) < share
    fast_rate = jnp.exp(jax.random.uniform(second, (CH, MODES), jnp.float32, math.log(1.0 / 50.0), math.log(1.0 / 30.0)))
    slow_rate = jnp.exp(jax.random.uniform(third, (CH, MODES), jnp.float32, math.log(0.3), math.log(2.3))) / L
    return jnp.where(fast, fast_rate, slow_rate).astype(jnp.float32)


def block_levels(rng, extent, cuts, least, high):
    factor_of = 1.0
    for position, blocks in cuts:
        steps = jax.random.uniform(jax.random.fold_in(jax.random.fold_in(rng, 6), position), (blocks,), jnp.float32, least / len(cuts), high / len(cuts))
        factor_of = factor_of * jnp.repeat(jnp.exp(steps), extent[position] // blocks).reshape((-1,) + (1,) * (len(extent) - 1 - position))
    return factor_of


def normal_values(own_key, shape, spread, limit, shards=(), kind=jnp.bfloat16):
    drawn = spread * jax.random.normal(own_key, shape, jnp.float32)
    if shards:
        drawn = drawn * block_levels(own_key, shape, shards, -0.22, 0.18)
    return jnp.clip(drawn, -limit, limit).astype(kind)


def setup_inputs(seed: int = 0) -> dict:
    streams_of = jax.random.split(jax.random.key(seed), 11)
    q_mr = normal_values(streams_of[0], (CH, L), 1.0, 6.0, ((0, 16), (1, 64)))
    k_mr = normal_values(streams_of[1], (CH, L), 1.0, 6.0, ((0, 16), (1, 64)))
    v_mr = draw_v_mr(jax.random.fold_in(streams_of[10], 71), 0)
    mr_taps = normal_values(streams_of[3], (TAPS, CH), TAPS ** -0.5, 0.5, ((1, 16),))
    norm_gain = jnp.clip(0.5 + 1.0 * jax.random.uniform(streams_of[4], (CH,), jnp.float32) ** block_levels(streams_of[4], (CH,), ((0, 16),), -0.2, 0.2), 0.5, 1.5)
    q_li = normal_values(streams_of[5], (CH, L), 1.0, 6.0, ((0, 16), (1, 64)))
    k_li = normal_values(streams_of[6], (CH, L), 1.0, 6.0, ((0, 16), (1, 64)))
    rates = draw_rates(jax.random.fold_in(streams_of[10], 71), 0)
    residues = normal_values(streams_of[8], (CH, MODES), 0.35, 2.0, ((0, 16),), jnp.float32)
    skip = jnp.clip(0.5 + 1.0 * jax.random.uniform(streams_of[9], (CH,), jnp.float32) ** block_levels(streams_of[9], (CH,), ((0, 16),), -0.2, 0.2), 0.5, 1.5)
    return dict(q_mr=q_mr, k_mr=k_mr, v_mr=v_mr, mr_taps=mr_taps, norm_gain=norm_gain, q_li=q_li, k_li=k_li, rates=rates, residues=residues, skip=skip)


group_width = 8

def split_rows(x):
    return x.reshape(CH // group_width, group_width, x.shape[1]).transpose(0, 2, 1)

def split_taps(x):
    return x.reshape(x.shape[0], CH // group_width, group_width).transpose(1, 0, 2)

def split_params(x):
    return x.reshape((CH // group_width, group_width) + x.shape[1:])

def mr_group(args):
    q_part, k_part, v_part, tap_part = args
    a_mr = (k_part.astype(jnp.float32) * v_part.astype(jnp.float32)).astype(jnp.bfloat16)
    a_mr = lax.optimization_barrier(a_mr).astype(jnp.float32)
    size = 2 * L
    spectrum = jnp.fft.rfft(a_mr, n=size, axis=0) * jnp.fft.rfft(tap_part.astype(jnp.float32), n=size, axis=0)
    mr_out = jnp.fft.irfft(spectrum, n=size, axis=0)[:L]
    return q_part.astype(jnp.float32) * mr_out

def reference(q_mr, k_mr, v_mr, mr_taps, norm_gain, q_li, k_li, rates, residues, skip):
    gated = lax.map(mr_group, (split_rows(q_mr), split_rows(k_mr), split_rows(v_mr), split_taps(mr_taps)))
    total = lax.optimization_barrier(jnp.sum(gated * gated, axis=(0, 2)))
    inv_rms = lax.rsqrt(total / CH + 1e-05)

    def li_group(args):
        gated_part, k_part, q_part, gain_part, rate_part, residue_part, skip_part = args
        v_li = (k_part.astype(jnp.float32) * gated_part * inv_rms[:, None] * gain_part[None, :]).astype(jnp.bfloat16)
        v_li = lax.optimization_barrier(v_li).astype(jnp.float32)
        times = jnp.arange(L, dtype=jnp.float32)
        weight = residue_part * jnp.sqrt(rate_part)
        filt = lax.optimization_barrier(jnp.sum(jnp.exp(-times[:, None, None] * rate_part[None]) * weight[None], axis=2))
        size = 2 * L
        spectrum = jnp.fft.rfft(v_li, n=size, axis=0) * jnp.fft.rfft(filt, n=size, axis=0)
        long_out = jnp.fft.irfft(spectrum, n=size, axis=0)[:L] + skip_part[None, :] * v_li
        long_out = lax.optimization_barrier(long_out.astype(jnp.bfloat16)).astype(jnp.float32)
        return (q_part.astype(jnp.float32) * long_out).astype(jnp.bfloat16)
    mixed = lax.map(li_group, (gated, split_rows(k_li), split_rows(q_li), split_params(norm_gain), split_params(rates), split_params(residues), split_params(skip)))
    return mixed.transpose(0, 2, 1).reshape(CH, L)
```

```python
import functools

import jax
import jax.numpy as jnp
from jax import lax
from jax.experimental import pallas as pl
from jax.experimental.pallas import tpu as pltpu
from jax.sharding import PartitionSpec as P

MESH = pl.DeviceIdType.MESH
F32 = jnp.float32
BF16 = jnp.bfloat16

CHANS = 64
ROWS = 512
HALF = 256
TAPS = 128
MODES = 16
LANES = 128


def packed(block):
    block = block.astype(F32)
    return jnp.concatenate([block[:, :HALF], block[:, HALF:]], axis=0).T


def kernel(
    group,
    q_mr,
    k_mr,
    v_mr,
    taps,
    gain,
    q_li,
    k_li,
    rates,
    residues,
    skip,
    out,
    in5,
    taps_in,
    gain_in,
    rates_in,
    residues_in,
    skip_in,
    a_own,
    rim,
    xs,
    far,
    tap_rows,
    wide,
    rate_rows,
    weight_rows,
    lift,
    filt,
    decay8,
    tail8,
    mr,
    sums_own,
    sums,
    vs,
    inner,
    state_own,
    states_z,
    total_own,
    states_y,
    result,
    in_sem,
    rim_sem,
    sums_send,
    sums_recv,
    z_send,
    z_recv,
    y_send,
    y_recv,
    out_sem,
):
    n_ctx, n_ch = lax.axis_size("ctx"), lax.axis_size("ch")
    n_y = n_ctx // group
    ctx, ch = lax.axis_index("ctx"), lax.axis_index("ch")
    place, plane = lax.rem(ctx, group), lax.div(ctx, group)

    rim[...] = jnp.zeros_like(rim)
    states_y[...] = jnp.zeros_like(states_y)

    barrier = pltpu.get_barrier_semaphore()

    def greet(device):
        pl.semaphore_signal(barrier, inc=1, device_id=device, device_id_type=MESH)

    @pl.when(ctx > 0)
    def _():
        greet({"ctx": ctx - 1, "ch": ch})

    @pl.when(ctx < n_ctx - 1)
    def _():
        greet({"ctx": ctx + 1, "ch": ch})

    for k in range(1, n_ch):
        greet({"ctx": ctx, "ch": lax.rem(ch + k, n_ch)})
    for k in range(1, group):
        greet({"ctx": plane * group + lax.rem(place + k, group), "ch": ch})
    for k in range(1, n_y):
        greet({"ctx": lax.rem(plane + k, n_y) * group + place, "ch": ch})

    loads = [
        pltpu.make_async_copy(src, dst, in_sem.at[i])
        for i, (src, dst) in enumerate(
            [
                (k_mr, in5.at[0]),
                (v_mr, in5.at[1]),
                (taps, taps_in),
                (rates, rates_in),
                (residues, residues_in),
                (q_mr, in5.at[2]),
                (k_li, in5.at[3]),
                (q_li, in5.at[4]),
                (gain, gain_in),
                (skip, skip_in),
            ]
        )
    ]
    for load in loads:
        load.start()

    lane = lax.broadcasted_iota(jnp.int32, (1, LANES), 1)
    first_half = lane < CHANS

    loads[0].wait()
    loads[1].wait()
    a = (in5[0].astype(F32) * in5[1].astype(F32)).astype(BF16)
    a_own[...] = a[:, ROWS - TAPS :]
    a_t = packed(a)
    xs[TAPS:, :] = a_t
    xs[:TAPS, :] = jnp.where(first_half, 0.0, pltpu.roll(a_t[HALF - TAPS :], CHANS, 1))
    far[TAPS:, :] = jnp.zeros((CHANS, LANES), F32)

    for load in loads[2:]:
        load.wait()
    tap_half = taps_in[...].astype(F32)
    tap_rows[...] = jnp.concatenate([tap_half, tap_half], axis=0).T

    def doubled(ref):
        wide[...] = jnp.zeros_like(wide)
        wide[:, :CHANS] = ref[...]
        return wide[...] + pltpu.roll(wide[...], CHANS, 1)

    rate = doubled(rates_in)
    weight = doubled(residues_in) * jnp.sqrt(rate)
    rate_rows[...] = rate
    weight_rows[...] = weight

    def doubled_row(ref):
        wide[...] = jnp.zeros_like(wide)
        wide[:1, :CHANS] = ref[...]
        return (wide[...] + pltpu.roll(wide[...], CHANS, 1))[:1]

    gain_row = doubled_row(gain_in)
    skip_row = doubled_row(skip_in)

    ends = jnp.where(ctx > 0, 1, 0) + jnp.where(ctx < n_ctx - 1, 1, 0)
    pl.semaphore_wait(barrier, n_ch - 1 + group - 1 + n_y - 1 + ends)

    def send_rim():
        return pltpu.make_async_remote_copy(
            src_ref=a_own,
            dst_ref=rim,
            send_sem=rim_sem.at[0],
            recv_sem=rim_sem.at[1],
            device_id={"ctx": ctx + 1, "ch": ch},
            device_id_type=MESH,
        )

    @pl.when(ctx < n_ctx - 1)
    def _():
        send_rim().start()

    def tap_step(i, acc):
        base = TAPS - 8 * i
        for p in range(8):
            acc = acc + xs[pl.ds(base - p, HALF), :] * tap_rows[pl.ds(8 * i + p, 1), :]
        return acc

    mr[...] = lax.fori_loop(0, TAPS // 8, tap_step, jnp.zeros((HALF, LANES), F32))

    times = lax.broadcasted_iota(jnp.int32, (HALF, LANES), 0).astype(F32)
    filt[...] = jnp.zeros_like(filt)

    @pl.loop(0, MODES)
    def _(r):
        term = jnp.exp(-rate_rows[pl.ds(r, 1), :] * times) * weight_rows[pl.ds(r, 1), :]
        lift[r] = term
        filt[...] += term

    offset8 = lax.broadcasted_iota(jnp.int32, (1, 8, LANES), 1).astype(F32)
    decay8[...] = jnp.broadcast_to(jnp.exp(rate * -8.0)[:, None, :], (MODES, 8, LANES))
    tail8[...] = jnp.exp(-rate[:, None, :] * (7.0 - offset8))

    q_t = packed(in5[2])
    k_t = packed(in5[3])

    @pl.when(ctx > 0)
    def _():
        send_rim().wait_recv()

    rim_now = rim[...].astype(F32)
    later = jnp.where(first_half, pltpu.roll(rim_now, CHANS, 1), 0.0)
    far[:TAPS, :] = jnp.concatenate([rim_now, later], axis=0).T

    def far_step(i, acc):
        base = TAPS - 8 * i
        for p in range(8):
            acc = acc + far[pl.ds(base - p, CHANS), :] * tap_rows[pl.ds(8 * i + p, 1), :]
        return acc

    reach = lax.fori_loop(0, TAPS // 8, far_step, jnp.zeros((CHANS, LANES), F32))
    mr[:CHANS, :] += jnp.where(first_half, reach, 0.0)
    mr[CHANS:TAPS, :] += jnp.where(first_half, pltpu.roll(reach, CHANS, 1), 0.0)

    gated = q_t * mr[...]
    squares = (gated * gated).T
    mine = jnp.concatenate(
        [
            jnp.sum(squares[:CHANS], axis=0, keepdims=True),
            jnp.sum(squares[CHANS:], axis=0, keepdims=True),
        ],
        axis=0,
    )
    sums_own[...] = mine
    sums[ch] = mine

    def send_sums(peer, slot):
        return pltpu.make_async_remote_copy(
            src_ref=sums_own,
            dst_ref=sums.at[slot],
            send_sem=sums_send.at[peer],
            recv_sem=sums_recv.at[slot],
            device_id={"ctx": ctx, "ch": peer},
            device_id_type=MESH,
        )

    for k in range(1, n_ch):
        send_sums(lax.rem(ch + k, n_ch), ch).start()
    raised = k_t * gated
    for k in range(1, n_ch):
        peer = lax.rem(ch + k, n_ch)
        send_sums(peer, peer).wait_recv()

    total = sums[0]
    for k in range(1, n_ch):
        total = total + sums[k]
    inv = lax.rsqrt(total / (n_ch * CHANS) + 1e-05)
    inv_t = jnp.concatenate(
        [
            jnp.broadcast_to(inv[:1], (CHANS, HALF)),
            jnp.broadcast_to(inv[1:], (CHANS, HALF)),
        ],
        axis=0,
    ).T
    v = (raised * inv_t * gain_row).astype(BF16).astype(F32)
    vs[:HALF, :] = jnp.zeros((HALF, LANES), F32)
    vs[HALF:, :] = v

    keep = decay8[...]
    acc = jnp.broadcast_to(v[None, :8], (MODES, 8, LANES))
    for i in range(1, HALF // 8):
        acc = acc * keep + v[None, 8 * i : 8 * i + 8]
    ends_half = jnp.sum(acc * tail8[...], axis=1)
    decay_half = jnp.exp(rate * -float(HALF))
    aged = jnp.where(first_half, ends_half * decay_half, ends_half)
    state = aged + pltpu.roll(aged, CHANS, 1)
    from_first = pltpu.roll(ends_half, CHANS, 1)

    def folded(x):
        return jnp.where(first_half, x[:8], x[8:])

    state_own[...] = folded(state)
    states_z[place] = folded(state)

    def send_z(peer, slot):
        return pltpu.make_async_remote_copy(
            src_ref=state_own,
            dst_ref=states_z.at[slot],
            send_sem=z_send.at[peer],
            recv_sem=z_recv.at[slot],
            device_id={"ctx": plane * group + peer, "ch": ch},
            device_id_type=MESH,
        )

    for k in range(1, group):
        send_z(lax.rem(place + k, group), place).start()

    inner[...] = skip_row * v
    block = 64
    for b in range(HALF // block):
        low = b * block

        def filt_step(i, acc, low=low):
            base = HALF - 8 * i
            for p in range(8):
                acc = acc + vs[pl.ds(base - p, HALF - low), :] * filt[pl.ds(low + 8 * i + p, 1), :]
            return acc

        inner[low:, :] += lax.fori_loop(
            0, block // 8, filt_step, jnp.zeros((HALF - low, LANES), F32)
        )
    ql_t = packed(in5[4])
    rate_folded = folded(rate)
    decay_one = jnp.exp(rate_folded * -float(ROWS))
    decay_plane = jnp.exp(rate_folded * -float(ROWS * group))
    decay_place = jnp.exp(rate_folded * (place.astype(F32) * -float(ROWS)))

    for k in range(1, group):
        peer = lax.rem(place + k, group)
        send_z(peer, peer).wait_recv()
    run = jnp.zeros((8, LANES), F32)
    before = jnp.zeros((8, LANES), F32)
    for k in range(group):
        before = jnp.where(place == k, run, before)
        run = run * decay_one + states_z[k]
    total_own[...] = run

    def send_y(peer, slot):
        return pltpu.make_async_remote_copy(
            src_ref=total_own,
            dst_ref=states_y.at[slot],
            send_sem=y_send.at[peer],
            recv_sem=y_recv.at[slot],
            device_id={"ctx": peer * group + place, "ch": ch},
            device_id_type=MESH,
        )

    for k in range(1, n_y):

        @pl.when(plane + k < n_y)
        def _(k=k):
            send_y(plane + k, plane).start()

    for k in range(1, n_y):

        @pl.when(plane - k >= 0)
        def _(k=k):
            send_y(plane - k, plane - k).wait_recv()

    carry = jnp.zeros((8, LANES), F32)
    for k in range(n_y - 1):
        carry = jnp.where(plane > k, carry * decay_plane + states_y[k], carry)
    carry = before + decay_place * carry

    low = jnp.where(first_half, carry, 0.0)
    high = jnp.where(first_half, 0.0, carry)
    carry = jnp.concatenate(
        [low + pltpu.roll(low, CHANS, 1), high + pltpu.roll(high, CHANS, 1)], axis=0
    )
    carry = jnp.where(first_half, carry, carry * decay_half + from_first)
    carry = carry * jnp.exp(-rate)
    acc = inner[...]
    for r in range(MODES):
        acc = acc + lift[r] * carry[r : r + 1]
    mixed = (ql_t * acc.astype(BF16).astype(F32)).T.astype(BF16)
    result[:, :HALF] = mixed[:CHANS]
    result[:, HALF:] = mixed[CHANS:]
    store = pltpu.make_async_copy(result, out, out_sem)
    store.start()

    @pl.when(ctx < n_ctx - 1)
    def _():
        send_rim().wait_send()

    for k in range(1, n_ch):
        send_sums(lax.rem(ch + k, n_ch), ch).wait_send()
    for k in range(1, group):
        send_z(lax.rem(place + k, group), place).wait_send()
    for k in range(1, n_y):

        @pl.when(plane + k < n_y)
        def _(k=k):
            send_y(plane + k, plane).wait_send()

    store.wait()


def build(mesh, group):
    n_ctx, n_ch = mesh.shape["ctx"], mesh.shape["ch"]
    n_y = n_ctx // group

    def per_device(q_mr, k_mr, v_mr, taps, gain, q_li, k_li, rates, residues, skip):
        dma = pltpu.SemaphoreType.DMA
        any_spec = pl.BlockSpec(memory_space=pl.ANY)
        return pl.pallas_call(
            functools.partial(kernel, group),
            out_shape=jax.ShapeDtypeStruct((CHANS, ROWS), BF16),
            in_specs=[any_spec] * 10,
            out_specs=any_spec,
            scratch_shapes=[
                pltpu.VMEM((5, CHANS, ROWS), BF16),
                pltpu.VMEM((CHANS, TAPS), BF16),
                pltpu.VMEM((1, CHANS), F32),
                pltpu.VMEM((MODES, CHANS), F32),
                pltpu.VMEM((MODES, CHANS), F32),
                pltpu.VMEM((1, CHANS), F32),
                pltpu.VMEM((CHANS, TAPS), BF16),
                pltpu.VMEM((CHANS, TAPS), BF16),
                pltpu.VMEM((TAPS + HALF, LANES), F32),
                pltpu.VMEM((TAPS + CHANS, LANES), F32),
                pltpu.VMEM((TAPS, LANES), F32),
                pltpu.VMEM((MODES, LANES), F32),
                pltpu.VMEM((MODES, LANES), F32),
                pltpu.VMEM((MODES, LANES), F32),
                pltpu.VMEM((MODES, HALF, LANES), F32),
                pltpu.VMEM((HALF, LANES), F32),
                pltpu.VMEM((MODES, 8, LANES), F32),
                pltpu.VMEM((MODES, 8, LANES), F32),
                pltpu.VMEM((HALF, LANES), F32),
                pltpu.VMEM((2, HALF), F32),
                pltpu.VMEM((n_ch, 2, HALF), F32),
                pltpu.VMEM((2 * HALF, LANES), F32),
                pltpu.VMEM((HALF, LANES), F32),
                pltpu.VMEM((8, LANES), F32),
                pltpu.VMEM((group, 8, LANES), F32),
                pltpu.VMEM((8, LANES), F32),
                pltpu.VMEM((n_y, 8, LANES), F32),
                pltpu.VMEM((CHANS, ROWS), BF16),
                dma((10,)),
                dma((2,)),
                dma((n_ch,)),
                dma((n_ch,)),
                dma((group,)),
                dma((group,)),
                dma((n_y,)),
                dma((n_y,)),
                dma,
            ],
            compiler_params=pltpu.CompilerParams(collective_id=0, has_side_effects=True),
            name="hyena_pair",
        )(
            q_mr,
            k_mr,
            v_mr,
            taps.T,
            gain.reshape(1, CHANS),
            q_li,
            k_li,
            rates.T,
            residues.T,
            skip.reshape(1, CHANS),
        )

    placed = (
        P("ch", "ctx"),
        P("ch", "ctx"),
        P("ch", "ctx"),
        P(None, "ch"),
        P("ch"),
        P("ch", "ctx"),
        P("ch", "ctx"),
        P("ch", None),
        P("ch", None),
        P("ch"),
    )
    return jax.shard_map(
        per_device, mesh=mesh, in_specs=placed, out_specs=P("ch", "ctx"), check_vma=False
    )


def solution(mesh):
    return build(mesh, 8)
```

```python
import functools

import jax
import jax.numpy as jnp
from jax import lax
from jax.experimental import pallas as pl
from jax.experimental.pallas import tpu as pltpu
from jax.sharding import PartitionSpec as P

MESH = pl.DeviceIdType.MESH
F32 = jnp.float32
BF16 = jnp.bfloat16

CHANS = 64
ROWS = 512
HALF = 256
TAPS = 128
MODES = 16
LANES = 128


def packed(block):
    block = block.astype(F32)
    return jnp.concatenate([block[:, :HALF], block[:, HALF:]], axis=0).T


def kernel(
    group,
    q_mr,
    k_mr,
    v_mr,
    taps,
    gain,
    q_li,
    k_li,
    rates,
    residues,
    skip,
    out,
    in5,
    taps_in,
    gain_in,
    rates_in,
    residues_in,
    skip_in,
    tails,
    a_own,
    rim,
    xs,
    far,
    tap_rows,
    wide,
    rate_rows,
    weight_rows,
    lift,
    filt,
    decay8,
    tail8,
    mr,
    sums_own,
    sums,
    vs,
    inner,
    state_own,
    states_z,
    total_own,
    states_y,
    result,
    in_sem,
    rim_sem,
    sums_send,
    sums_recv,
    z_send,
    z_recv,
    y_send,
    y_recv,
    out_sem,
    far_ready,
    first_ready,
    ends_ready,
    early_own,
    early,
    first_own,
    first,
    raised_own,
    raised_in,
    main_own,
    main_in,
    early_send,
    early_recv,
    first_send,
    first_recv,
    raised_sem,
    main_sem,
):
    n_ctx, n_ch = lax.axis_size("ctx"), lax.axis_size("ch")
    n_y = n_ctx // group
    ctx, ch = lax.axis_index("ctx"), lax.axis_index("ch")
    place, plane = lax.rem(ctx, group), lax.div(ctx, group)
    core = lax.rem(ctx, 2)
    n_z = group // 2
    z = lax.div(place, 2)

    def at(dz, dcore):
        return 2 * lax.rem(z + dz, n_z) + lax.rem(core + dcore, 2)

    others = [(dz, dc) for dz in range(n_z) for dc in (0, 1) if (dz, dc) != (0, 0)]
    others = others[1:] + others[:1]

    hasty = (z == 2) & (core == 0) if n_z == 4 else None

    def column_sums(gated):
        squares = (gated * gated).T
        return jnp.concatenate(
            [
                jnp.sum(squares[:CHANS], axis=0, keepdims=True),
                jnp.sum(squares[CHANS:], axis=0, keepdims=True),
            ],
            axis=0,
        )

    def send_early(peer, slot):
        return pltpu.make_async_remote_copy(
            src_ref=early_own,
            dst_ref=early.at[slot],
            send_sem=early_send.at[peer],
            recv_sem=early_recv.at[slot],
            device_id={"ctx": ctx, "ch": peer},
            device_id_type=MESH,
        )

    def send_first(dcore, peer, slot):
        return pltpu.make_async_remote_copy(
            src_ref=first_own,
            dst_ref=first.at[slot],
            send_sem=first_send.at[dcore * n_ch + peer],
            recv_sem=first_recv.at[slot],
            device_id={"ctx": plane * group + dcore, "ch": peer},
            device_id_type=MESH,
        )

    def send_plain(src, dst, sem, dcore):
        return pltpu.make_async_remote_copy(
            src_ref=src,
            dst_ref=dst,
            send_sem=sem.at[dcore],
            recv_sem=sem.at[2],
            device_id={"ctx": plane * group + dcore, "ch": ch},
            device_id_type=MESH,
        )

    rim[...] = jnp.zeros_like(rim)
    states_y[...] = jnp.zeros_like(states_y)

    barrier = pltpu.get_barrier_semaphore()

    def greet(device):
        pl.semaphore_signal(barrier, inc=1, device_id=device, device_id_type=MESH)

    def in_group(dz, dcore):
        return {"ctx": plane * group + at(dz, dcore), "ch": ch}

    @pl.when((place == 0) & (plane > 0))
    def _():
        greet({"ctx": ctx - 1, "ch": ch})

    @pl.when(z > 0)
    def _():
        for dc in (1, 0):
            greet(in_group(n_z - 1, dc))

    @pl.when(z < n_z - 1)
    def _():
        for dc in (0, 1):
            greet(in_group(1, dc))

    greet(in_group(0, 1))
    for k in range(1, n_ch):
        greet({"ctx": ctx, "ch": lax.rem(ch + k, n_ch)})
    for k in range(1, n_y):
        greet({"ctx": lax.rem(plane + k, n_y) * group + place, "ch": ch})

    tail = pl.ds(ROWS - TAPS, TAPS)
    loads = [
        pltpu.make_async_copy(src, dst, in_sem.at[i])
        for i, (src, dst) in enumerate(
            [
                (k_mr.at[:, tail], tails.at[0]),
                (v_mr.at[:, tail], tails.at[1]),
                (k_mr, in5.at[0]),
                (v_mr, in5.at[1]),
                (taps, taps_in),
                (rates, rates_in),
                (residues, residues_in),
                (q_mr, in5.at[2]),
                (k_li, in5.at[3]),
                (q_li, in5.at[4]),
                (gain, gain_in),
                (skip, skip_in),
            ]
        )
    ]
    for load in loads:
        load.start()

    lane = lax.broadcasted_iota(jnp.int32, (1, LANES), 1)
    first_half = lane < CHANS

    loads[0].wait()
    loads[1].wait()
    a_own[...] = (tails[0].astype(F32) * tails[1].astype(F32)).astype(BF16)
    loads[2].wait()
    loads[3].wait()
    a = (in5[0].astype(F32) * in5[1].astype(F32)).astype(BF16)
    a_t = packed(a)
    xs[TAPS:, :] = a_t
    xs[:TAPS, :] = jnp.where(first_half, 0.0, pltpu.roll(a_t[HALF - TAPS :], CHANS, 1))
    far[TAPS:, :] = jnp.zeros((CHANS, LANES), F32)

    for load in loads[4:]:
        load.wait()
    tap_half = taps_in[...].astype(F32)
    tap_rows[...] = jnp.concatenate([tap_half, tap_half], axis=0).T

    def doubled(ref):
        wide[...] = jnp.zeros_like(wide)
        wide[:, :CHANS] = ref[...]
        return wide[...] + pltpu.roll(wide[...], CHANS, 1)

    rate = doubled(rates_in)
    weight = doubled(residues_in) * jnp.sqrt(rate)
    rate_rows[...] = rate
    weight_rows[...] = weight

    def doubled_row(ref):
        wide[...] = jnp.zeros_like(wide)
        wide[:1, :CHANS] = ref[...]
        return (wide[...] + pltpu.roll(wide[...], CHANS, 1))[:1]

    gain_row = doubled_row(gain_in)
    skip_row = doubled_row(skip_in)

    q_t = packed(in5[2])
    k_t = packed(in5[3])

    def tap_step(i, acc):
        base = TAPS - 8 * i
        for p in range(8):
            acc = acc + xs[pl.ds(base - p, HALF), :] * tap_rows[pl.ds(8 * i + p, 1), :]
        return acc

    def own_taps():
        mr[...] = lax.fori_loop(0, TAPS // 8, tap_step, jnp.zeros((HALF, LANES), F32))

    if n_z == 4:
        pl.when(hasty)(own_taps)

    greeted = n_ch - 1 + n_y - 1 + 1
    greeted += jnp.where(z > 0, 2, 0) + jnp.where(z < n_z - 1, 2, 0)
    greeted += jnp.where((place == group - 1) & (plane < n_y - 1), 1, 0)
    pl.semaphore_wait(barrier, greeted)

    def send_rim():
        return pltpu.make_async_remote_copy(
            src_ref=a_own,
            dst_ref=rim,
            send_sem=rim_sem.at[0],
            recv_sem=rim_sem.at[1],
            device_id={"ctx": ctx + 1, "ch": ch},
            device_id_type=MESH,
        )

    @pl.when(ctx < n_ctx - 1)
    def _():
        send_rim().start()

    def tell(sem, dz, dcore):
        pl.semaphore_signal(sem, inc=1, device_id=in_group(dz, dcore), device_id_type=MESH)

    if n_z == 4:

        @pl.when(z == 0)
        def _():
            tell(first_ready, 1, 0)

        @pl.when(z == 1)
        def _():
            pl.semaphore_wait(first_ready, 1)
            tell(far_ready, 1, 0)
            tell(ends_ready, 1, core)

        @pl.when(z == 2)
        def _():
            tell(far_ready, n_z - 1, 0)

        @pl.when(hasty)
        def _():
            gated = q_t * mr[...]
            mine = column_sums(gated)
            early_own[...] = mine
            early[ch] = mine
            for k in range(1, n_ch):
                send_early(lax.rem(ch + k, n_ch), ch).start()

    if n_z == 4:
        pl.when(jnp.logical_not(hasty))(own_taps)
    else:
        own_taps()

    @pl.when(ctx > 0)
    def _():
        send_rim().wait_recv()

    rim_now = rim[...].astype(F32)
    later = jnp.where(first_half, pltpu.roll(rim_now, CHANS, 1), 0.0)
    far[:TAPS, :] = jnp.concatenate([rim_now, later], axis=0).T

    def far_step(i, acc):
        base = TAPS - 8 * i
        for p in range(8):
            acc = acc + far[pl.ds(base - p, CHANS), :] * tap_rows[pl.ds(8 * i + p, 1), :]
        return acc

    reach = lax.fori_loop(0, TAPS // 8, far_step, jnp.zeros((CHANS, LANES), F32))
    mr[:CHANS, :] += jnp.where(first_half, reach, 0.0)
    mr[CHANS:TAPS, :] += jnp.where(first_half, pltpu.roll(reach, CHANS, 1), 0.0)

    gated = q_t * mr[...]
    mine = column_sums(gated)
    sums_own[...] = mine
    sums[ch] = mine

    def send_sums(peer, slot):
        return pltpu.make_async_remote_copy(
            src_ref=sums_own,
            dst_ref=sums.at[slot],
            send_sem=sums_send.at[peer],
            recv_sem=sums_recv.at[slot],
            device_id={"ctx": ctx, "ch": peer},
            device_id_type=MESH,
        )

    for k in range(1, n_ch):
        send_sums(lax.rem(ch + k, n_ch), ch).start()
    raised = k_t * gated

    if n_z == 4:

        @pl.when(hasty)
        def _():
            pl.semaphore_wait(ends_ready, 2)
            first_own[...] = mine[:1, :TAPS]
            for dcore in (0, 1):
                for k in range(n_ch):
                    send_first(dcore, lax.rem(ch + k, n_ch), ch).start()
            raised_own[...] = jnp.where(
                first_half, raised[:CHANS], pltpu.roll(raised[CHANS:TAPS], CHANS, 1)
            ).astype(BF16)
            for dcore in (0, 1):
                send_plain(raised_own, raised_in, raised_sem, dcore).start()

    if n_z == 4:

        @pl.when(z == 1)
        def _():
            pl.semaphore_wait(far_ready, 1)
            tell(far_ready, n_z - 1, 0)

        @pl.when(z == 2)
        def _():
            pl.semaphore_wait(far_ready, 1)
            tell(far_ready, 1, 0)

    times = lax.broadcasted_iota(jnp.int32, (HALF, LANES), 0).astype(F32)
    filt[...] = jnp.zeros_like(filt)

    @pl.loop(0, MODES)
    def _(r):
        term = jnp.exp(-rate_rows[pl.ds(r, 1), :] * times) * weight_rows[pl.ds(r, 1), :]
        lift[r] = term
        filt[...] += term

    offset8 = lax.broadcasted_iota(jnp.int32, (1, 8, LANES), 1).astype(F32)
    decay8[...] = jnp.broadcast_to(jnp.exp(rate * -8.0)[:, None, :], (MODES, 8, LANES))
    tail8[...] = jnp.exp(-rate[:, None, :] * (7.0 - offset8))

    def normed(sums):
        total = sums[0]
        for k in range(1, n_ch):
            total = total + sums[k]
        inv = lax.rsqrt(total / (n_ch * CHANS) + 1e-05)
        inv_t = jnp.concatenate(
            [
                jnp.broadcast_to(inv[:1], (CHANS, HALF)),
                jnp.broadcast_to(inv[1:], (CHANS, HALF)),
            ],
            axis=0,
        ).T
        return (raised * inv_t * gain_row).astype(BF16).astype(F32)

    def ends_of(v):
        keep = decay8[...]
        acc = jnp.broadcast_to(v[None, :8], (MODES, 8, LANES))
        for i in range(1, v.shape[0] // 8):
            acc = acc * keep + v[None, 8 * i : 8 * i + 8]
        return jnp.sum(acc * tail8[...], axis=1)

    def folded(x):
        return jnp.where(first_half, x[:8], x[8:])

    def joined(aged):
        return folded(aged + pltpu.roll(aged, CHANS, 1))

    decay_half = jnp.exp(rate * -float(HALF))

    if n_z == 4:

        @pl.when(hasty)
        def _():
            for k in range(1, n_ch):
                peer = lax.rem(ch + k, n_ch)
                send_early(peer, peer).wait_recv()
            row = lax.broadcasted_iota(jnp.int32, (HALF, LANES), 0)
            v = jnp.where(first_half & (row < TAPS), 0.0, normed(early))
            ends = ends_of(v)
            main_own[...] = joined(jnp.where(first_half, ends * decay_half, ends))
            for dcore in (0, 1):
                send_plain(main_own, main_in, main_sem, dcore).start()

    for k in range(1, n_ch):
        peer = lax.rem(ch + k, n_ch)
        send_sums(peer, peer).wait_recv()

    v = normed(sums)
    vs[:HALF, :] = jnp.zeros((HALF, LANES), F32)
    vs[HALF:, :] = v

    ends_half = ends_of(v)
    state = joined(jnp.where(first_half, ends_half * decay_half, ends_half))
    from_first = pltpu.roll(ends_half, CHANS, 1)
    state_own[...] = state
    states_z[place] = state

    def send_z(peer, slot):
        return pltpu.make_async_remote_copy(
            src_ref=state_own,
            dst_ref=states_z.at[slot],
            send_sem=z_send.at[peer],
            recv_sem=z_recv.at[slot],
            device_id={"ctx": plane * group + peer, "ch": ch},
            device_id_type=MESH,
        )

    if n_z == 4:

        @pl.when((z == 0) | (z == n_z - 1))
        def _():
            pl.semaphore_wait(far_ready, 1)

    def for_others(act, sending):
        for step in others:
            peer = at(*step)
            if n_z == 4 and step[0] == 2:
                skip_it = hasty if sending else (z == 0) & (lax.rem(peer, 2) == 0)

                @pl.when(jnp.logical_not(skip_it))
                def _(peer=peer):
                    act(send_z(peer, place if sending else peer))

            else:
                act(send_z(peer, place if sending else peer))

    for_others(lambda copy: copy.start(), True)

    inner[...] = skip_row * v
    block = 64
    for b in range(HALF // block):
        low = b * block

        def filt_step(i, acc, low=low):
            base = HALF - 8 * i
            for p in range(8):
                acc = acc + vs[pl.ds(base - p, HALF - low), :] * filt[pl.ds(low + 8 * i + p, 1), :]
            return acc

        inner[low:, :] += lax.fori_loop(
            0, block // 8, filt_step, jnp.zeros((HALF - low, LANES), F32)
        )
    ql_t = packed(in5[4])
    rate_folded = folded(rate)
    decay_one = jnp.exp(rate_folded * -float(ROWS))
    decay_plane = jnp.exp(rate_folded * -float(ROWS * group))
    decay_place = jnp.exp(rate_folded * (place.astype(F32) * -float(ROWS)))

    if n_z == 4:

        @pl.when(z == 0)
        def _():
            for k in range(n_ch):
                send_first(0, k, k).wait_recv()
            total = first[0]
            for k in range(1, n_ch):
                total = total + first[k]
            inv = lax.rsqrt(total / (n_ch * CHANS) + 1e-05)
            inv_t = jnp.concatenate(
                [
                    jnp.broadcast_to(inv, (CHANS, LANES)),
                    jnp.broadcast_to(pltpu.roll(inv, CHANS, 1), (CHANS, LANES)),
                ],
                axis=0,
            ).T[:CHANS]
            send_plain(raised_own, raised_in, raised_sem, 0).wait_recv()
            v = (raised_in[...].astype(F32) * inv_t * gain_row).astype(BF16).astype(F32)
            age = jnp.where(first_half, float(ROWS - CHANS), float(ROWS - TAPS))
            added = joined(ends_of(v) * jnp.exp(-rate * age))
            send_plain(main_own, main_in, main_sem, 0).wait_recv()
            states_z[4] = main_in[...] + added

    for_others(lambda copy: copy.wait_recv(), False)
    run = jnp.zeros((8, LANES), F32)
    before = jnp.zeros((8, LANES), F32)
    for k in range(group):
        before = jnp.where(place == k, run, before)
        run = run * decay_one + states_z[k]
    total_own[...] = run

    def send_y(peer, slot):
        return pltpu.make_async_remote_copy(
            src_ref=total_own,
            dst_ref=states_y.at[slot],
            send_sem=y_send.at[peer],
            recv_sem=y_recv.at[slot],
            device_id={"ctx": peer * group + place, "ch": ch},
            device_id_type=MESH,
        )

    for k in range(1, n_y):

        @pl.when(plane + k < n_y)
        def _(k=k):
            send_y(plane + k, plane).start()

    for k in range(1, n_y):

        @pl.when(plane - k >= 0)
        def _(k=k):
            send_y(plane - k, plane - k).wait_recv()

    carry = jnp.zeros((8, LANES), F32)
    for k in range(n_y - 1):
        carry = jnp.where(plane > k, carry * decay_plane + states_y[k], carry)
    carry = before + decay_place * carry

    low = jnp.where(first_half, carry, 0.0)
    high = jnp.where(first_half, 0.0, carry)
    carry = jnp.concatenate(
        [low + pltpu.roll(low, CHANS, 1), high + pltpu.roll(high, CHANS, 1)], axis=0
    )
    carry = jnp.where(first_half, carry, carry * decay_half + from_first)
    carry = carry * jnp.exp(-rate)
    acc = inner[...]
    for r in range(MODES):
        acc = acc + lift[r] * carry[r : r + 1]
    mixed = (ql_t * acc.astype(BF16).astype(F32)).T.astype(BF16)
    result[:, :HALF] = mixed[:CHANS]
    result[:, HALF:] = mixed[CHANS:]
    out[...] = result[...]

    @pl.when(ctx < n_ctx - 1)
    def _():
        send_rim().wait_send()

    for k in range(1, n_ch):
        send_sums(lax.rem(ch + k, n_ch), ch).wait_send()
    for_others(lambda copy: copy.wait_send(), True)
    if n_z == 4:

        @pl.when(hasty)
        def _():
            for k in range(1, n_ch):
                send_early(lax.rem(ch + k, n_ch), ch).wait_send()
            for dcore in (0, 1):
                for k in range(n_ch):
                    send_first(dcore, lax.rem(ch + k, n_ch), ch).wait_send()
                send_plain(raised_own, raised_in, raised_sem, dcore).wait_send()
                send_plain(main_own, main_in, main_sem, dcore).wait_send()

    for k in range(1, n_y):

        @pl.when(plane + k < n_y)
        def _(k=k):
            send_y(plane + k, plane).wait_send()


def build(mesh, group):
    n_ctx, n_ch = mesh.shape["ctx"], mesh.shape["ch"]
    n_y = n_ctx // group

    def per_device(q_mr, k_mr, v_mr, taps, gain, q_li, k_li, rates, residues, skip):
        dma = pltpu.SemaphoreType.DMA
        any_spec = pl.BlockSpec(memory_space=pl.ANY)
        return pl.pallas_call(
            functools.partial(kernel, group),
            out_shape=pltpu.VMEM((CHANS, ROWS), BF16),
            in_specs=[any_spec] * 10,
            out_specs=pl.BlockSpec(memory_space=pltpu.VMEM),
            scratch_shapes=[
                pltpu.VMEM((5, CHANS, ROWS), BF16),
                pltpu.VMEM((CHANS, TAPS), BF16),
                pltpu.VMEM((1, CHANS), F32),
                pltpu.VMEM((MODES, CHANS), F32),
                pltpu.VMEM((MODES, CHANS), F32),
                pltpu.VMEM((1, CHANS), F32),
                pltpu.VMEM((2, CHANS, TAPS), BF16),
                pltpu.VMEM((CHANS, TAPS), BF16),
                pltpu.VMEM((CHANS, TAPS), BF16),
                pltpu.VMEM((TAPS + HALF, LANES), F32),
                pltpu.VMEM((TAPS + CHANS, LANES), F32),
                pltpu.VMEM((TAPS, LANES), F32),
                pltpu.VMEM((MODES, LANES), F32),
                pltpu.VMEM((MODES, LANES), F32),
                pltpu.VMEM((MODES, LANES), F32),
                pltpu.VMEM((MODES, HALF, LANES), F32),
                pltpu.VMEM((HALF, LANES), F32),
                pltpu.VMEM((MODES, 8, LANES), F32),
                pltpu.VMEM((MODES, 8, LANES), F32),
                pltpu.VMEM((HALF, LANES), F32),
                pltpu.VMEM((2, HALF), F32),
                pltpu.VMEM((n_ch, 2, HALF), F32),
                pltpu.VMEM((2 * HALF, LANES), F32),
                pltpu.VMEM((HALF, LANES), F32),
                pltpu.VMEM((8, LANES), F32),
                pltpu.VMEM((group, 8, LANES), F32),
                pltpu.VMEM((8, LANES), F32),
                pltpu.VMEM((n_y, 8, LANES), F32),
                pltpu.VMEM((CHANS, ROWS), BF16),
                dma((12,)),
                dma((2,)),
                dma((n_ch,)),
                dma((n_ch,)),
                dma((group,)),
                dma((group,)),
                dma((n_y,)),
                dma((n_y,)),
                dma,
                pltpu.SemaphoreType.REGULAR,
                pltpu.SemaphoreType.REGULAR,
                pltpu.SemaphoreType.REGULAR,
                pltpu.VMEM((2, HALF), F32),
                pltpu.VMEM((n_ch, 2, HALF), F32),
                pltpu.VMEM((1, TAPS), F32),
                pltpu.VMEM((n_ch, 1, TAPS), F32),
                pltpu.VMEM((CHANS, LANES), BF16),
                pltpu.VMEM((CHANS, LANES), BF16),
                pltpu.VMEM((8, LANES), F32),
                pltpu.VMEM((8, LANES), F32),
                dma((n_ch,)),
                dma((n_ch,)),
                dma((2 * n_ch,)),
                dma((n_ch,)),
                dma((3,)),
                dma((3,)),
            ],
            compiler_params=pltpu.CompilerParams(collective_id=0, has_side_effects=True),
            name="hyena_pair",
        )(
            q_mr,
            k_mr,
            v_mr,
            taps.T,
            gain.reshape(1, CHANS),
            q_li,
            k_li,
            rates.T,
            residues.T,
            skip.reshape(1, CHANS),
        )

    placed = (
        P("ch", "ctx"),
        P("ch", "ctx"),
        P("ch", "ctx"),
        P(None, "ch"),
        P("ch"),
        P("ch", "ctx"),
        P("ch", "ctx"),
        P("ch", None),
        P("ch", None),
        P("ch"),
    )
    return jax.shard_map(
        per_device, mesh=mesh, in_specs=placed, out_specs=P("ch", "ctx"), check_vma=False
    )


def solution(mesh):
    return build(mesh, 8)
```

```python
import functools

import jax
import jax.numpy as jnp
from jax import lax
from jax.experimental import pallas as pl
from jax.experimental.pallas import tpu as pltpu
from jax.sharding import PartitionSpec as P

MESH = pl.DeviceIdType.MESH
F32 = jnp.float32
BF16 = jnp.bfloat16

CHANS = 64
ROWS = 512
HALF = 256
TAPS = 128
MODES = 16
LANES = 128


def packed(block):
    block = block.astype(F32)
    return jnp.concatenate([block[:, :HALF], block[:, HALF:]], axis=0).T


def kernel(
    group,
    q_mr,
    k_mr,
    v_mr,
    taps,
    gain,
    q_li,
    k_li,
    rates,
    residues,
    skip,
    out,
    in5,
    taps_in,
    gain_in,
    rates_in,
    residues_in,
    skip_in,
    tails,
    a_own,
    rim,
    xs,
    far,
    tap_rows,
    wide,
    rate_rows,
    weight_rows,
    lift,
    filt,
    decay8,
    tail8,
    mr,
    sums_own,
    sums,
    vs,
    inner,
    state_own,
    states_z,
    total_own,
    states_y,
    result,
    in_sem,
    rim_sem,
    sums_send,
    sums_recv,
    z_send,
    z_recv,
    y_send,
    y_recv,
    out_sem,
    far_ready,
    early_own,
    early,
    first_own,
    first,
    raised_own,
    raised_in,
    main_own,
    main_in,
    early_send,
    early_recv,
    first_send,
    first_recv,
    raised_sem,
    main_sem,
):
    n_ctx, n_ch = lax.axis_size("ctx"), lax.axis_size("ch")
    n_y = n_ctx // group
    ctx, ch = lax.axis_index("ctx"), lax.axis_index("ch")
    place, plane = lax.rem(ctx, group), lax.div(ctx, group)
    core = lax.rem(ctx, 2)
    n_z = group // 2
    z = lax.div(place, 2)

    def at(dz, dcore):
        return 2 * lax.rem(z + dz, n_z) + lax.rem(core + dcore, 2)

    others = [(dz, dc) for dz in range(n_z) for dc in (0, 1) if (dz, dc) != (0, 0)]
    others = others[1:] + others[:1]

    hasty = (z >= 2) & (core == 0) if n_z == 4 else None
    late = z - 2

    def column_sums(gated):
        squares = (gated * gated).T
        return jnp.concatenate(
            [
                jnp.sum(squares[:CHANS], axis=0, keepdims=True),
                jnp.sum(squares[CHANS:], axis=0, keepdims=True),
            ],
            axis=0,
        )

    def send_early(peer, slot):
        return pltpu.make_async_remote_copy(
            src_ref=early_own,
            dst_ref=early.at[slot],
            send_sem=early_send.at[peer],
            recv_sem=early_recv.at[slot],
            device_id={"ctx": ctx, "ch": peer},
            device_id_type=MESH,
        )

    def send_first(dcore, peer, slot):
        return pltpu.make_async_remote_copy(
            src_ref=first_own,
            dst_ref=first.at[slot],
            send_sem=first_send.at[dcore * n_ch + peer],
            recv_sem=first_recv.at[slot],
            device_id={"ctx": plane * group + dcore, "ch": peer},
            device_id_type=MESH,
        )

    def send_plain(src, dst, sem, dcore, slot):
        return pltpu.make_async_remote_copy(
            src_ref=src,
            dst_ref=dst.at[slot],
            send_sem=sem.at[dcore],
            recv_sem=sem.at[2 + slot],
            device_id={"ctx": plane * group + dcore, "ch": ch},
            device_id_type=MESH,
        )

    rim[...] = jnp.zeros_like(rim)
    states_y[...] = jnp.zeros_like(states_y)

    barrier = pltpu.get_barrier_semaphore()

    def greet(device):
        pl.semaphore_signal(barrier, inc=1, device_id=device, device_id_type=MESH)

    def in_group(dz, dcore):
        return {"ctx": plane * group + at(dz, dcore), "ch": ch}

    @pl.when((place == 0) & (plane > 0))
    def _():
        greet({"ctx": ctx - 1, "ch": ch})

    @pl.when(z > 0)
    def _():
        for dc in (1, 0):
            greet(in_group(n_z - 1, dc))

    @pl.when(z < n_z - 1)
    def _():
        for dc in (0, 1):
            greet(in_group(1, dc))

    if n_z == 4:

        @pl.when(z == 0)
        def _():
            for place_late in (6, 4):
                for k in range(n_ch):
                    greet({"ctx": plane * group + place_late, "ch": lax.rem(ch + k, n_ch)})

    greet(in_group(0, 1))
    for k in range(1, n_ch):
        greet({"ctx": ctx, "ch": lax.rem(ch + k, n_ch)})
    for k in range(1, n_y):
        greet({"ctx": lax.rem(plane + k, n_y) * group + place, "ch": ch})

    tail = pl.ds(ROWS - TAPS, TAPS)
    loads = [
        pltpu.make_async_copy(src, dst, in_sem.at[i])
        for i, (src, dst) in enumerate(
            [
                (k_mr.at[:, tail], tails.at[0]),
                (v_mr.at[:, tail], tails.at[1]),
                (k_mr, in5.at[0]),
                (v_mr, in5.at[1]),
                (taps, taps_in),
                (rates, rates_in),
                (residues, residues_in),
                (q_mr, in5.at[2]),
                (k_li, in5.at[3]),
                (q_li, in5.at[4]),
                (gain, gain_in),
                (skip, skip_in),
            ]
        )
    ]
    for load in loads:
        load.start()

    lane = lax.broadcasted_iota(jnp.int32, (1, LANES), 1)
    first_half = lane < CHANS

    loads[0].wait()
    loads[1].wait()
    a_own[...] = (tails[0].astype(F32) * tails[1].astype(F32)).astype(BF16)
    loads[2].wait()
    loads[3].wait()
    a = (in5[0].astype(F32) * in5[1].astype(F32)).astype(BF16)
    a_t = packed(a)
    xs[TAPS:, :] = a_t
    xs[:TAPS, :] = jnp.where(first_half, 0.0, pltpu.roll(a_t[HALF - TAPS :], CHANS, 1))
    far[TAPS:, :] = jnp.zeros((CHANS, LANES), F32)

    for load in loads[4:]:
        load.wait()
    tap_half = taps_in[...].astype(F32)
    tap_rows[...] = jnp.concatenate([tap_half, tap_half], axis=0).T

    def doubled(ref):
        wide[...] = jnp.zeros_like(wide)
        wide[:, :CHANS] = ref[...]
        return wide[...] + pltpu.roll(wide[...], CHANS, 1)

    rate = doubled(rates_in)
    weight = doubled(residues_in) * jnp.sqrt(rate)
    rate_rows[...] = rate
    weight_rows[...] = weight

    def doubled_row(ref):
        wide[...] = jnp.zeros_like(wide)
        wide[:1, :CHANS] = ref[...]
        return (wide[...] + pltpu.roll(wide[...], CHANS, 1))[:1]

    gain_row = doubled_row(gain_in)
    skip_row = doubled_row(skip_in)

    q_t = packed(in5[2])
    k_t = packed(in5[3])

    def tap_step(i, acc):
        base = TAPS - 8 * i
        for p in range(8):
            acc = acc + xs[pl.ds(base - p, HALF), :] * tap_rows[pl.ds(8 * i + p, 1), :]
        return acc

    def own_taps():
        mr[...] = lax.fori_loop(0, TAPS // 8, tap_step, jnp.zeros((HALF, LANES), F32))

    if n_z == 4:
        pl.when(hasty)(own_taps)

    greeted = n_ch - 1 + n_y - 1 + 1
    greeted += jnp.where(z > 0, 2, 0) + jnp.where(z < n_z - 1, 2, 0)
    greeted += jnp.where((place == group - 1) & (plane < n_y - 1), 1, 0)
    if n_z == 4:
        greeted += jnp.where(hasty, 2 * n_ch, 0)
    pl.semaphore_wait(barrier, greeted)

    def send_rim():
        return pltpu.make_async_remote_copy(
            src_ref=a_own,
            dst_ref=rim,
            send_sem=rim_sem.at[0],
            recv_sem=rim_sem.at[1],
            device_id={"ctx": ctx + 1, "ch": ch},
            device_id_type=MESH,
        )

    @pl.when(ctx < n_ctx - 1)
    def _():
        send_rim().start()

    def tell(sem, dz, dcore):
        pl.semaphore_signal(sem, inc=1, device_id=in_group(dz, dcore), device_id_type=MESH)

    if n_z == 4:

        @pl.when(z == 1)
        def _():
            tell(far_ready, 1, 0)

        @pl.when(z == 2)
        def _():
            tell(far_ready, n_z - 1, 0)

        @pl.when(hasty)
        def _():
            gated = q_t * mr[...]
            mine = column_sums(gated)
            early_own[...] = mine
            early[ch] = mine
            for k in range(1, n_ch):
                send_early(lax.rem(ch + k, n_ch), ch).start()

    if n_z == 4:
        pl.when(jnp.logical_not(hasty))(own_taps)
    else:
        own_taps()

    @pl.when(ctx > 0)
    def _():
        send_rim().wait_recv()

    rim_now = rim[...].astype(F32)
    later = jnp.where(first_half, pltpu.roll(rim_now, CHANS, 1), 0.0)
    far[:TAPS, :] = jnp.concatenate([rim_now, later], axis=0).T

    def far_step(i, acc):
        base = TAPS - 8 * i
        for p in range(8):
            acc = acc + far[pl.ds(base - p, CHANS), :] * tap_rows[pl.ds(8 * i + p, 1), :]
        return acc

    reach = lax.fori_loop(0, TAPS // 8, far_step, jnp.zeros((CHANS, LANES), F32))
    mr[:CHANS, :] += jnp.where(first_half, reach, 0.0)
    mr[CHANS:TAPS, :] += jnp.where(first_half, pltpu.roll(reach, CHANS, 1), 0.0)

    gated = q_t * mr[...]
    mine = column_sums(gated)
    sums_own[...] = mine
    sums[ch] = mine

    def send_sums(peer, slot):
        return pltpu.make_async_remote_copy(
            src_ref=sums_own,
            dst_ref=sums.at[slot],
            send_sem=sums_send.at[peer],
            recv_sem=sums_recv.at[slot],
            device_id={"ctx": ctx, "ch": peer},
            device_id_type=MESH,
        )

    for k in range(1, n_ch):
        send_sums(lax.rem(ch + k, n_ch), ch).start()
    raised = k_t * gated

    if n_z == 4:

        @pl.when(hasty)
        def _():
            first_own[...] = mine[:1, :TAPS]
            for dcore in (0, 1):
                for k in range(n_ch):
                    send_first(dcore, lax.rem(ch + k, n_ch), late * n_ch + ch).start()
            raised_own[...] = jnp.where(
                first_half, raised[:CHANS], pltpu.roll(raised[CHANS:TAPS], CHANS, 1)
            ).astype(BF16)
            for dcore in (0, 1):
                send_plain(raised_own, raised_in, raised_sem, dcore, late).start()

    if n_z == 4:

        @pl.when(z == 1)
        def _():
            pl.semaphore_wait(far_ready, 1)
            tell(far_ready, n_z - 1, 0)

        @pl.when(z == 2)
        def _():
            pl.semaphore_wait(far_ready, 1)
            tell(far_ready, 1, 0)

    times = lax.broadcasted_iota(jnp.int32, (HALF, LANES), 0).astype(F32)
    filt[...] = jnp.zeros_like(filt)

    @pl.loop(0, MODES)
    def _(r):
        term = jnp.exp(-rate_rows[pl.ds(r, 1), :] * times) * weight_rows[pl.ds(r, 1), :]
        lift[r] = term
        filt[...] += term

    offset8 = lax.broadcasted_iota(jnp.int32, (1, 8, LANES), 1).astype(F32)
    decay8[...] = jnp.broadcast_to(jnp.exp(rate * -8.0)[:, None, :], (MODES, 8, LANES))
    tail8[...] = jnp.exp(-rate[:, None, :] * (7.0 - offset8))

    def normed(sums):
        total = sums[0]
        for k in range(1, n_ch):
            total = total + sums[k]
        inv = lax.rsqrt(total / (n_ch * CHANS) + 1e-05)
        inv_t = jnp.concatenate(
            [
                jnp.broadcast_to(inv[:1], (CHANS, HALF)),
                jnp.broadcast_to(inv[1:], (CHANS, HALF)),
            ],
            axis=0,
        ).T
        return (raised * inv_t * gain_row).astype(BF16).astype(F32)

    def ends_of(v):
        keep = decay8[...]
        acc = jnp.broadcast_to(v[None, :8], (MODES, 8, LANES))
        for i in range(1, v.shape[0] // 8):
            acc = acc * keep + v[None, 8 * i : 8 * i + 8]
        return jnp.sum(acc * tail8[...], axis=1)

    def folded(x):
        return jnp.where(first_half, x[:8], x[8:])

    def joined(aged):
        return folded(aged + pltpu.roll(aged, CHANS, 1))

    decay_half = jnp.exp(rate * -float(HALF))

    if n_z == 4:

        @pl.when(hasty)
        def _():
            for k in range(1, n_ch):
                peer = lax.rem(ch + k, n_ch)
                send_early(peer, peer).wait_recv()
            row = lax.broadcasted_iota(jnp.int32, (HALF, LANES), 0)
            v = jnp.where(first_half & (row < TAPS), 0.0, normed(early))
            ends = ends_of(v)
            main_own[...] = joined(jnp.where(first_half, ends * decay_half, ends))
            for dcore in (0, 1):
                send_plain(main_own, main_in, main_sem, dcore, late).start()

    for k in range(1, n_ch):
        peer = lax.rem(ch + k, n_ch)
        send_sums(peer, peer).wait_recv()

    v = normed(sums)
    vs[:HALF, :] = jnp.zeros((HALF, LANES), F32)
    vs[HALF:, :] = v

    ends_half = ends_of(v)
    state = joined(jnp.where(first_half, ends_half * decay_half, ends_half))
    from_first = pltpu.roll(ends_half, CHANS, 1)
    state_own[...] = state
    states_z[place] = state

    def send_z(peer, slot):
        return pltpu.make_async_remote_copy(
            src_ref=state_own,
            dst_ref=states_z.at[slot],
            send_sem=z_send.at[peer],
            recv_sem=z_recv.at[slot],
            device_id={"ctx": plane * group + peer, "ch": ch},
            device_id_type=MESH,
        )

    if n_z == 4:

        @pl.when((z == 0) | (z == n_z - 1))
        def _():
            pl.semaphore_wait(far_ready, 1)

    def for_others(act, sending):
        for step in others:
            peer = at(*step)
            if n_z == 4 and step[0] > 0:
                replaced = (
                    hasty & (peer < 2) if sending else (z == 0) & (peer >= 4) & (lax.rem(peer, 2) == 0)
                )

                @pl.when(jnp.logical_not(replaced))
                def _(peer=peer):
                    act(send_z(peer, place if sending else peer))

            else:
                act(send_z(peer, place if sending else peer))

    for_others(lambda copy: copy.start(), True)

    inner[...] = skip_row * v
    block = 64
    for b in range(HALF // block):
        low = b * block

        def filt_step(i, acc, low=low):
            base = HALF - 8 * i
            for p in range(8):
                acc = acc + vs[pl.ds(base - p, HALF - low), :] * filt[pl.ds(low + 8 * i + p, 1), :]
            return acc

        inner[low:, :] += lax.fori_loop(
            0, block // 8, filt_step, jnp.zeros((HALF - low, LANES), F32)
        )
    ql_t = packed(in5[4])
    rate_folded = folded(rate)
    decay_one = jnp.exp(rate_folded * -float(ROWS))
    decay_plane = jnp.exp(rate_folded * -float(ROWS * group))
    decay_place = jnp.exp(rate_folded * (place.astype(F32) * -float(ROWS)))

    if n_z == 4:

        @pl.when(z == 0)
        def _():
            for slot in (1, 0):
                for k in range(n_ch):
                    send_first(0, k, slot * n_ch + k).wait_recv()
                total = first[slot * n_ch]
                for k in range(1, n_ch):
                    total = total + first[slot * n_ch + k]
                inv = lax.rsqrt(total / (n_ch * CHANS) + 1e-05)
                inv_t = jnp.concatenate(
                    [
                        jnp.broadcast_to(inv, (CHANS, LANES)),
                        jnp.broadcast_to(pltpu.roll(inv, CHANS, 1), (CHANS, LANES)),
                    ],
                    axis=0,
                ).T[:CHANS]
                send_plain(raised_own, raised_in, raised_sem, 0, slot).wait_recv()
                v = (raised_in[slot].astype(F32) * inv_t * gain_row).astype(BF16).astype(F32)
                age = jnp.where(first_half, float(ROWS - CHANS), float(ROWS - TAPS))
                added = joined(ends_of(v) * jnp.exp(-rate * age))
                send_plain(main_own, main_in, main_sem, 0, slot).wait_recv()
                states_z[4 + 2 * slot] = main_in[slot] + added

    for_others(lambda copy: copy.wait_recv(), False)
    run = jnp.zeros((8, LANES), F32)
    before = jnp.zeros((8, LANES), F32)
    for k in range(group):
        before = jnp.where(place == k, run, before)
        run = run * decay_one + states_z[k]
    total_own[...] = run

    def send_y(peer, slot):
        return pltpu.make_async_remote_copy(
            src_ref=total_own,
            dst_ref=states_y.at[slot],
            send_sem=y_send.at[peer],
            recv_sem=y_recv.at[slot],
            device_id={"ctx": peer * group + place, "ch": ch},
            device_id_type=MESH,
        )

    for k in range(1, n_y):

        @pl.when(plane + k < n_y)
        def _(k=k):
            send_y(plane + k, plane).start()

    for k in range(1, n_y):

        @pl.when(plane - k >= 0)
        def _(k=k):
            send_y(plane - k, plane - k).wait_recv()

    carry = jnp.zeros((8, LANES), F32)
    for k in range(n_y - 1):
        carry = jnp.where(plane > k, carry * decay_plane + states_y[k], carry)
    carry = before + decay_place * carry

    low = jnp.where(first_half, carry, 0.0)
    high = jnp.where(first_half, 0.0, carry)
    carry = jnp.concatenate(
        [low + pltpu.roll(low, CHANS, 1), high + pltpu.roll(high, CHANS, 1)], axis=0
    )
    carry = jnp.where(first_half, carry, carry * decay_half + from_first)
    carry = carry * jnp.exp(-rate)
    acc = inner[...]
    for r in range(MODES):
        acc = acc + lift[r] * carry[r : r + 1]
    mixed = (ql_t * acc.astype(BF16).astype(F32)).T.astype(BF16)
    result[:, :HALF] = mixed[:CHANS]
    result[:, HALF:] = mixed[CHANS:]
    out[...] = result[...]

    @pl.when(ctx < n_ctx - 1)
    def _():
        send_rim().wait_send()

    for k in range(1, n_ch):
        send_sums(lax.rem(ch + k, n_ch), ch).wait_send()
    for_others(lambda copy: copy.wait_send(), True)
    if n_z == 4:

        @pl.when(hasty)
        def _():
            for k in range(1, n_ch):
                send_early(lax.rem(ch + k, n_ch), ch).wait_send()
            for dcore in (0, 1):
                for k in range(n_ch):
                    send_first(dcore, lax.rem(ch + k, n_ch), late * n_ch + ch).wait_send()
                send_plain(raised_own, raised_in, raised_sem, dcore, late).wait_send()
                send_plain(main_own, main_in, main_sem, dcore, late).wait_send()

    for k in range(1, n_y):

        @pl.when(plane + k < n_y)
        def _(k=k):
            send_y(plane + k, plane).wait_send()


def build(mesh, group):
    n_ctx, n_ch = mesh.shape["ctx"], mesh.shape["ch"]
    n_y = n_ctx // group

    def per_device(q_mr, k_mr, v_mr, taps, gain, q_li, k_li, rates, residues, skip):
        dma = pltpu.SemaphoreType.DMA
        any_spec = pl.BlockSpec(memory_space=pl.ANY)
        return pl.pallas_call(
            functools.partial(kernel, group),
            out_shape=pltpu.VMEM((CHANS, ROWS), BF16),
            in_specs=[any_spec] * 10,
            out_specs=pl.BlockSpec(memory_space=pltpu.VMEM),
            scratch_shapes=[
                pltpu.VMEM((5, CHANS, ROWS), BF16),
                pltpu.VMEM((CHANS, TAPS), BF16),
                pltpu.VMEM((1, CHANS), F32),
                pltpu.VMEM((MODES, CHANS), F32),
                pltpu.VMEM((MODES, CHANS), F32),
                pltpu.VMEM((1, CHANS), F32),
                pltpu.VMEM((2, CHANS, TAPS), BF16),
                pltpu.VMEM((CHANS, TAPS), BF16),
                pltpu.VMEM((CHANS, TAPS), BF16),
                pltpu.VMEM((TAPS + HALF, LANES), F32),
                pltpu.VMEM((TAPS + CHANS, LANES), F32),
                pltpu.VMEM((TAPS, LANES), F32),
                pltpu.VMEM((MODES, LANES), F32),
                pltpu.VMEM((MODES, LANES), F32),
                pltpu.VMEM((MODES, LANES), F32),
                pltpu.VMEM((MODES, HALF, LANES), F32),
                pltpu.VMEM((HALF, LANES), F32),
                pltpu.VMEM((MODES, 8, LANES), F32),
                pltpu.VMEM((MODES, 8, LANES), F32),
                pltpu.VMEM((HALF, LANES), F32),
                pltpu.VMEM((2, HALF), F32),
                pltpu.VMEM((n_ch, 2, HALF), F32),
                pltpu.VMEM((2 * HALF, LANES), F32),
                pltpu.VMEM((HALF, LANES), F32),
                pltpu.VMEM((8, LANES), F32),
                pltpu.VMEM((group, 8, LANES), F32),
                pltpu.VMEM((8, LANES), F32),
                pltpu.VMEM((n_y, 8, LANES), F32),
                pltpu.VMEM((CHANS, ROWS), BF16),
                dma((12,)),
                dma((2,)),
                dma((n_ch,)),
                dma((n_ch,)),
                dma((group,)),
                dma((group,)),
                dma((n_y,)),
                dma((n_y,)),
                dma,
                pltpu.SemaphoreType.REGULAR,
                pltpu.VMEM((2, HALF), F32),
                pltpu.VMEM((n_ch, 2, HALF), F32),
                pltpu.VMEM((1, TAPS), F32),
                pltpu.VMEM((2 * n_ch, 1, TAPS), F32),
                pltpu.VMEM((CHANS, LANES), BF16),
                pltpu.VMEM((2, CHANS, LANES), BF16),
                pltpu.VMEM((8, LANES), F32),
                pltpu.VMEM((2, 8, LANES), F32),
                dma((n_ch,)),
                dma((n_ch,)),
                dma((2 * n_ch,)),
                dma((2 * n_ch,)),
                dma((4,)),
                dma((4,)),
            ],
            compiler_params=pltpu.CompilerParams(collective_id=0, has_side_effects=True),
            name="hyena_pair",
        )(
            q_mr,
            k_mr,
            v_mr,
            taps.T,
            gain.reshape(1, CHANS),
            q_li,
            k_li,
            rates.T,
            residues.T,
            skip.reshape(1, CHANS),
        )

    placed = (
        P("ch", "ctx"),
        P("ch", "ctx"),
        P("ch", "ctx"),
        P(None, "ch"),
        P("ch"),
        P("ch", "ctx"),
        P("ch", "ctx"),
        P("ch", None),
        P("ch", None),
        P("ch"),
    )
    return jax.shard_map(
        per_device, mesh=mesh, in_specs=placed, out_specs=P("ch", "ctx"), check_vma=False
    )


def solution(mesh):
    return build(mesh, 8)
```

```python
import functools

import jax
import jax.numpy as jnp
from jax import lax
from jax.experimental import pallas as pl
from jax.experimental.pallas import tpu as pltpu
from jax.sharding import PartitionSpec as P

MESH = pl.DeviceIdType.MESH
F32 = jnp.float32
BF16 = jnp.bfloat16

CHANS = 64
ROWS = 512
HALF = 256
TAPS = 128
MODES = 16
LANES = 128


def packed(block):
    block = block.astype(F32)
    return jnp.concatenate([block[:, :HALF], block[:, HALF:]], axis=0).T


def kernel(
    group,
    q_mr,
    k_mr,
    v_mr,
    taps,
    gain,
    q_li,
    k_li,
    rates,
    residues,
    skip,
    out,
    in5,
    taps_in,
    gain_in,
    rates_in,
    residues_in,
    skip_in,
    tails,
    a_own,
    rim,
    xs,
    far,
    tap_rows,
    wide,
    rate_rows,
    weight_rows,
    lift,
    filt,
    decay8,
    tail8,
    mr,
    sums_own,
    sums,
    vs,
    inner,
    state_own,
    states_z,
    total_own,
    states_y,
    result,
    in_sem,
    rim_sem,
    sums_send,
    sums_recv,
    z_send,
    z_recv,
    y_send,
    y_recv,
    out_sem,
    far_ready,
    early_own,
    early,
    first_own,
    first,
    raised_own,
    raised_in,
    main_own,
    main_in,
    early_send,
    early_recv,
    first_send,
    first_recv,
    raised_sem,
    main_sem,
):
    n_ctx, n_ch = lax.axis_size("ctx"), lax.axis_size("ch")
    n_y = n_ctx // group
    ctx, ch = lax.axis_index("ctx"), lax.axis_index("ch")
    place, plane = lax.rem(ctx, group), lax.div(ctx, group)
    core = lax.rem(ctx, 2)
    n_z = group // 2
    z = lax.div(place, 2)

    def at(dz, dcore):
        return 2 * lax.rem(z + dz, n_z) + lax.rem(core + dcore, 2)

    others = [(dz, dc) for dz in range(n_z) for dc in (0, 1) if (dz, dc) != (0, 0)]
    others = others[1:] + others[:1]

    hasty = (z >= 2) & (core == 0) if n_z == 4 else None
    late = z - 2

    def column_sums(gated):
        squares = (gated * gated).T
        return jnp.concatenate(
            [
                jnp.sum(squares[:CHANS], axis=0, keepdims=True),
                jnp.sum(squares[CHANS:], axis=0, keepdims=True),
            ],
            axis=0,
        )

    def send_early(peer, slot):
        return pltpu.make_async_remote_copy(
            src_ref=early_own,
            dst_ref=early.at[slot],
            send_sem=early_send.at[peer],
            recv_sem=early_recv.at[slot],
            device_id={"ctx": ctx, "ch": peer},
            device_id_type=MESH,
        )

    def send_first(dcore, peer, slot):
        return pltpu.make_async_remote_copy(
            src_ref=first_own,
            dst_ref=first.at[slot],
            send_sem=first_send.at[dcore * n_ch + peer],
            recv_sem=first_recv.at[slot],
            device_id={"ctx": plane * group + dcore, "ch": peer},
            device_id_type=MESH,
        )

    def send_plain(src, dst, sem, dcore, slot):
        return pltpu.make_async_remote_copy(
            src_ref=src,
            dst_ref=dst.at[slot],
            send_sem=sem.at[dcore],
            recv_sem=sem.at[2 + slot],
            device_id={"ctx": plane * group + dcore, "ch": ch},
            device_id_type=MESH,
        )

    rim[...] = jnp.zeros_like(rim)
    states_y[...] = jnp.zeros_like(states_y)

    barrier = pltpu.get_barrier_semaphore()

    def greet(device):
        pl.semaphore_signal(barrier, inc=1, device_id=device, device_id_type=MESH)

    def in_group(dz, dcore):
        return {"ctx": plane * group + at(dz, dcore), "ch": ch}

    @pl.when((place == 0) & (plane > 0))
    def _():
        greet({"ctx": ctx - 1, "ch": ch})

    @pl.when(z > 0)
    def _():
        for dc in (1, 0):
            greet(in_group(n_z - 1, dc))

    @pl.when(z < n_z - 1)
    def _():
        for dc in (0, 1):
            greet(in_group(1, dc))

    if n_z == 4:

        @pl.when(z == 0)
        def _():
            for place_late in (6, 4):
                for k in range(n_ch):
                    greet({"ctx": plane * group + place_late, "ch": lax.rem(ch + k, n_ch)})

    greet(in_group(0, 1))
    for k in range(1, n_ch):
        greet({"ctx": ctx, "ch": lax.rem(ch + k, n_ch)})
    for k in range(1, n_y):
        greet({"ctx": lax.rem(plane + k, n_y) * group + place, "ch": ch})

    tail = pl.ds(ROWS - TAPS, TAPS)
    loads = [
        pltpu.make_async_copy(src, dst, in_sem.at[i])
        for i, (src, dst) in enumerate(
            [
                (k_mr.at[:, tail], tails.at[0]),
                (v_mr.at[:, tail], tails.at[1]),
                (k_mr, in5.at[0]),
                (v_mr, in5.at[1]),
                (taps, taps_in),
                (rates, rates_in),
                (residues, residues_in),
                (q_mr, in5.at[2]),
                (k_li, in5.at[3]),
                (q_li, in5.at[4]),
                (gain, gain_in),
                (skip, skip_in),
            ]
        )
    ]
    for load in loads:
        load.start()

    lane = lax.broadcasted_iota(jnp.int32, (1, LANES), 1)
    first_half = lane < CHANS

    loads[0].wait()
    loads[1].wait()
    a_own[...] = (tails[0].astype(F32) * tails[1].astype(F32)).astype(BF16)
    loads[2].wait()
    loads[3].wait()
    a = (in5[0].astype(F32) * in5[1].astype(F32)).astype(BF16)
    a_t = packed(a)
    xs[TAPS:, :] = a_t
    xs[:TAPS, :] = jnp.where(first_half, 0.0, pltpu.roll(a_t[HALF - TAPS :], CHANS, 1))
    far[TAPS:, :] = jnp.zeros((CHANS, LANES), F32)

    for load in loads[4:]:
        load.wait()
    tap_half = taps_in[...].astype(F32)
    tap_rows[...] = jnp.concatenate([tap_half, tap_half], axis=0).T

    def doubled(ref):
        wide[...] = jnp.zeros_like(wide)
        wide[:, :CHANS] = ref[...]
        return wide[...] + pltpu.roll(wide[...], CHANS, 1)

    rate = doubled(rates_in)
    weight = doubled(residues_in) * jnp.sqrt(rate)
    rate_rows[...] = rate
    weight_rows[...] = weight

    def doubled_row(ref):
        wide[...] = jnp.zeros_like(wide)
        wide[:1, :CHANS] = ref[...]
        return (wide[...] + pltpu.roll(wide[...], CHANS, 1))[:1]

    gain_row = doubled_row(gain_in)
    skip_row = doubled_row(skip_in)

    q_t = packed(in5[2])
    k_t = packed(in5[3])

    def tap_step(i, acc):
        base = TAPS - 8 * i
        for p in range(8):
            acc = acc + xs[pl.ds(base - p, HALF), :] * tap_rows[pl.ds(8 * i + p, 1), :]
        return acc

    def own_taps():
        mr[...] = lax.fori_loop(0, TAPS // 8, tap_step, jnp.zeros((HALF, LANES), F32))

    if n_z == 4:
        pl.when(hasty)(own_taps)

    greeted = n_ch - 1 + n_y - 1 + 1
    greeted += jnp.where(z > 0, 2, 0) + jnp.where(z < n_z - 1, 2, 0)
    greeted += jnp.where((place == group - 1) & (plane < n_y - 1), 1, 0)
    if n_z == 4:
        greeted += jnp.where(hasty, 2 * n_ch, 0)
    pl.semaphore_wait(barrier, greeted)

    def send_rim():
        return pltpu.make_async_remote_copy(
            src_ref=a_own,
            dst_ref=rim,
            send_sem=rim_sem.at[0],
            recv_sem=rim_sem.at[1],
            device_id={"ctx": ctx + 1, "ch": ch},
            device_id_type=MESH,
        )

    @pl.when(ctx < n_ctx - 1)
    def _():
        send_rim().start()

    def tell(sem, dz, dcore):
        pl.semaphore_signal(sem, inc=1, device_id=in_group(dz, dcore), device_id_type=MESH)

    if n_z == 4:

        @pl.when(z == 1)
        def _():
            tell(far_ready, 1, 0)

        @pl.when(z == 2)
        def _():
            tell(far_ready, n_z - 1, 0)

        @pl.when(hasty)
        def _():
            gated = q_t * mr[...]
            mine = column_sums(gated)
            early_own[...] = mine
            early[ch] = mine
            for k in range(1, n_ch):
                send_early(lax.rem(ch + k, n_ch), ch).start()

    if n_z == 4:
        pl.when(jnp.logical_not(hasty))(own_taps)
    else:
        own_taps()

    @pl.when(ctx > 0)
    def _():
        send_rim().wait_recv()

    rim_now = rim[...].astype(F32)
    later = jnp.where(first_half, pltpu.roll(rim_now, CHANS, 1), 0.0)
    far[:TAPS, :] = jnp.concatenate([rim_now, later], axis=0).T

    def far_step(i, acc):
        base = TAPS - 8 * i
        for p in range(8):
            acc = acc + far[pl.ds(base - p, CHANS), :] * tap_rows[pl.ds(8 * i + p, 1), :]
        return acc

    reach = lax.fori_loop(0, TAPS // 8, far_step, jnp.zeros((CHANS, LANES), F32))
    mr[:CHANS, :] += jnp.where(first_half, reach, 0.0)
    mr[CHANS:TAPS, :] += jnp.where(first_half, pltpu.roll(reach, CHANS, 1), 0.0)

    gated = q_t * mr[...]
    mine = column_sums(gated)
    sums_own[...] = mine
    sums[ch] = mine

    def send_sums(peer, slot):
        return pltpu.make_async_remote_copy(
            src_ref=sums_own,
            dst_ref=sums.at[slot],
            send_sem=sums_send.at[peer],
            recv_sem=sums_recv.at[slot],
            device_id={"ctx": ctx, "ch": peer},
            device_id_type=MESH,
        )

    for k in range(1, n_ch):
        send_sums(lax.rem(ch + k, n_ch), ch).start()
    raised = k_t * gated

    if n_z == 4:

        @pl.when(hasty)
        def _():
            first_own[...] = mine[:1, :TAPS]
            for dcore in (0, 1):
                for k in range(n_ch):
                    send_first(dcore, lax.rem(ch + k, n_ch), late * n_ch + ch).start()
            raised_own[...] = jnp.where(
                first_half, raised[:CHANS], pltpu.roll(raised[CHANS:TAPS], CHANS, 1)
            ).astype(BF16)
            for dcore in (0, 1):
                send_plain(raised_own, raised_in, raised_sem, dcore, late).start()

    if n_z == 4:

        @pl.when(z == 1)
        def _():
            pl.semaphore_wait(far_ready, 1)
            tell(far_ready, n_z - 1, 0)

        @pl.when(z == 2)
        def _():
            pl.semaphore_wait(far_ready, 1)
            tell(far_ready, 1, 0)

    times = lax.broadcasted_iota(jnp.int32, (HALF, LANES), 0).astype(F32)
    filt[...] = jnp.zeros_like(filt)

    @pl.loop(0, MODES)
    def _(r):
        term = jnp.exp(-rate_rows[pl.ds(r, 1), :] * times) * weight_rows[pl.ds(r, 1), :]
        lift[r] = term
        filt[...] += term

    offset8 = lax.broadcasted_iota(jnp.int32, (1, 8, LANES), 1).astype(F32)
    decay8[...] = jnp.broadcast_to(jnp.exp(rate * -8.0)[:, None, :], (MODES, 8, LANES))
    tail8[...] = jnp.exp(-rate[:, None, :] * (7.0 - offset8))

    def normed(sums):
        total = sums[0]
        for k in range(1, n_ch):
            total = total + sums[k]
        inv = lax.rsqrt(total / (n_ch * CHANS) + 1e-05)
        inv_t = jnp.concatenate(
            [
                jnp.broadcast_to(inv[:1], (CHANS, HALF)),
                jnp.broadcast_to(inv[1:], (CHANS, HALF)),
            ],
            axis=0,
        ).T
        return (raised * inv_t * gain_row).astype(BF16).astype(F32)

    def ends_of(v):
        keep = decay8[...]
        acc = jnp.broadcast_to(v[None, :8], (MODES, 8, LANES))
        for i in range(1, v.shape[0] // 8):
            acc = acc * keep + v[None, 8 * i : 8 * i + 8]
        return jnp.sum(acc * tail8[...], axis=1)

    def folded(x):
        return jnp.where(first_half, x[:8], x[8:])

    def joined(aged):
        return folded(aged + pltpu.roll(aged, CHANS, 1))

    decay_half = jnp.exp(rate * -float(HALF))

    if n_z == 4:

        @pl.when(hasty)
        def _():
            for k in range(1, n_ch):
                peer = lax.rem(ch + k, n_ch)
                send_early(peer, peer).wait_recv()
            row = lax.broadcasted_iota(jnp.int32, (HALF, LANES), 0)
            v = jnp.where(first_half & (row < TAPS), 0.0, normed(early))
            ends = ends_of(v)
            main_own[...] = joined(jnp.where(first_half, ends * decay_half, ends))
            for dcore in (0, 1):
                send_plain(main_own, main_in, main_sem, dcore, late).start()

    for k in range(1, n_ch):
        peer = lax.rem(ch + k, n_ch)
        send_sums(peer, peer).wait_recv()

    v = normed(sums)
    vs[:HALF, :] = jnp.zeros((HALF, LANES), F32)
    vs[HALF:, :] = v

    ends_half = ends_of(v)
    state = joined(jnp.where(first_half, ends_half * decay_half, ends_half))
    from_first = pltpu.roll(ends_half, CHANS, 1)
    state_own[...] = state
    states_z[place] = state

    def send_z(peer, slot):
        return pltpu.make_async_remote_copy(
            src_ref=state_own,
            dst_ref=states_z.at[slot],
            send_sem=z_send.at[peer],
            recv_sem=z_recv.at[slot],
            device_id={"ctx": plane * group + peer, "ch": ch},
            device_id_type=MESH,
        )

    if n_z == 4:

        @pl.when((z == 0) | (z == n_z - 1))
        def _():
            pl.semaphore_wait(far_ready, 1)

    def for_others(act, sending):
        for step in others:
            peer = at(*step)
            if n_z == 4 and step[0] > 0:
                replaced = (
                    hasty & (peer < 2) if sending else (z == 0) & (peer >= 4) & (lax.rem(peer, 2) == 0)
                )

                @pl.when(jnp.logical_not(replaced))
                def _(peer=peer):
                    act(send_z(peer, place if sending else peer))

            else:
                act(send_z(peer, place if sending else peer))

    for_others(lambda copy: copy.start(), True)

    def own_filter():
        inner[...] = skip_row * v
        block = 64
        for b in range(HALF // block):
            low = b * block

            def filt_step(i, acc, low=low):
                base = HALF - 8 * i
                for p in range(8):
                    acc = acc + vs[pl.ds(base - p, HALF - low), :] * filt[pl.ds(low + 8 * i + p, 1), :]
                return acc

            inner[low:, :] += lax.fori_loop(
                0, block // 8, filt_step, jnp.zeros((HALF - low, LANES), F32)
            )

    waited_for = (plane > 0) & (plane < n_y - 1)
    pl.when(jnp.logical_not(waited_for))(own_filter)
    rate_folded = folded(rate)
    decay_one = jnp.exp(rate_folded * -float(ROWS))
    decay_plane = jnp.exp(rate_folded * -float(ROWS * group))
    decay_place = jnp.exp(rate_folded * (place.astype(F32) * -float(ROWS)))

    if n_z == 4:

        @pl.when(z == 0)
        def _():
            for slot in (1, 0):
                for k in range(n_ch):
                    send_first(0, k, slot * n_ch + k).wait_recv()
                total = first[slot * n_ch]
                for k in range(1, n_ch):
                    total = total + first[slot * n_ch + k]
                inv = lax.rsqrt(total / (n_ch * CHANS) + 1e-05)
                inv_t = jnp.concatenate(
                    [
                        jnp.broadcast_to(inv, (CHANS, LANES)),
                        jnp.broadcast_to(pltpu.roll(inv, CHANS, 1), (CHANS, LANES)),
                    ],
                    axis=0,
                ).T[:CHANS]
                send_plain(raised_own, raised_in, raised_sem, 0, slot).wait_recv()
                v = (raised_in[slot].astype(F32) * inv_t * gain_row).astype(BF16).astype(F32)
                age = jnp.where(first_half, float(ROWS - CHANS), float(ROWS - TAPS))
                added = joined(ends_of(v) * jnp.exp(-rate * age))
                send_plain(main_own, main_in, main_sem, 0, slot).wait_recv()
                states_z[4 + 2 * slot] = main_in[slot] + added

    for_others(lambda copy: copy.wait_recv(), False)
    run = jnp.zeros((8, LANES), F32)
    before = jnp.zeros((8, LANES), F32)
    for k in range(group):
        before = jnp.where(place == k, run, before)
        run = run * decay_one + states_z[k]
    total_own[...] = run

    def send_y(peer, slot):
        return pltpu.make_async_remote_copy(
            src_ref=total_own,
            dst_ref=states_y.at[slot],
            send_sem=y_send.at[peer],
            recv_sem=y_recv.at[slot],
            device_id={"ctx": peer * group + place, "ch": ch},
            device_id_type=MESH,
        )

    for k in range(1, n_y):

        @pl.when(plane + k < n_y)
        def _(k=k):
            send_y(plane + k, plane).start()

    pl.when(waited_for)(own_filter)
    ql_t = packed(in5[4])
    for k in range(1, n_y):

        @pl.when(plane - k >= 0)
        def _(k=k):
            send_y(plane - k, plane - k).wait_recv()

    carry = jnp.zeros((8, LANES), F32)
    for k in range(n_y - 1):
        carry = jnp.where(plane > k, carry * decay_plane + states_y[k], carry)
    carry = before + decay_place * carry

    low = jnp.where(first_half, carry, 0.0)
    high = jnp.where(first_half, 0.0, carry)
    carry = jnp.concatenate(
        [low + pltpu.roll(low, CHANS, 1), high + pltpu.roll(high, CHANS, 1)], axis=0
    )
    carry = jnp.where(first_half, carry, carry * decay_half + from_first)
    carry = carry * jnp.exp(-rate)
    acc = inner[...]
    for r in range(MODES):
        acc = acc + lift[r] * carry[r : r + 1]
    mixed = (ql_t * acc.astype(BF16).astype(F32)).T.astype(BF16)
    result[:, :HALF] = mixed[:CHANS]
    result[:, HALF:] = mixed[CHANS:]
    out[...] = result[...]

    @pl.when(ctx < n_ctx - 1)
    def _():
        send_rim().wait_send()

    for k in range(1, n_ch):
        send_sums(lax.rem(ch + k, n_ch), ch).wait_send()
    for_others(lambda copy: copy.wait_send(), True)
    if n_z == 4:

        @pl.when(hasty)
        def _():
            for k in range(1, n_ch):
                send_early(lax.rem(ch + k, n_ch), ch).wait_send()
            for dcore in (0, 1):
                for k in range(n_ch):
                    send_first(dcore, lax.rem(ch + k, n_ch), late * n_ch + ch).wait_send()
                send_plain(raised_own, raised_in, raised_sem, dcore, late).wait_send()
                send_plain(main_own, main_in, main_sem, dcore, late).wait_send()

    for k in range(1, n_y):

        @pl.when(plane + k < n_y)
        def _(k=k):
            send_y(plane + k, plane).wait_send()


def build(mesh, group):
    n_ctx, n_ch = mesh.shape["ctx"], mesh.shape["ch"]
    n_y = n_ctx // group

    def per_device(q_mr, k_mr, v_mr, taps, gain, q_li, k_li, rates, residues, skip):
        dma = pltpu.SemaphoreType.DMA
        any_spec = pl.BlockSpec(memory_space=pl.ANY)
        return pl.pallas_call(
            functools.partial(kernel, group),
            out_shape=pltpu.VMEM((CHANS, ROWS), BF16),
            in_specs=[any_spec] * 10,
            out_specs=pl.BlockSpec(memory_space=pltpu.VMEM),
            scratch_shapes=[
                pltpu.VMEM((5, CHANS, ROWS), BF16),
                pltpu.VMEM((CHANS, TAPS), BF16),
                pltpu.VMEM((1, CHANS), F32),
                pltpu.VMEM((MODES, CHANS), F32),
                pltpu.VMEM((MODES, CHANS), F32),
                pltpu.VMEM((1, CHANS), F32),
                pltpu.VMEM((2, CHANS, TAPS), BF16),
                pltpu.VMEM((CHANS, TAPS), BF16),
                pltpu.VMEM((CHANS, TAPS), BF16),
                pltpu.VMEM((TAPS + HALF, LANES), F32),
                pltpu.VMEM((TAPS + CHANS, LANES), F32),
                pltpu.VMEM((TAPS, LANES), F32),
                pltpu.VMEM((MODES, LANES), F32),
                pltpu.VMEM((MODES, LANES), F32),
                pltpu.VMEM((MODES, LANES), F32),
                pltpu.VMEM((MODES, HALF, LANES), F32),
                pltpu.VMEM((HALF, LANES), F32),
                pltpu.VMEM((MODES, 8, LANES), F32),
                pltpu.VMEM((MODES, 8, LANES), F32),
                pltpu.VMEM((HALF, LANES), F32),
                pltpu.VMEM((2, HALF), F32),
                pltpu.VMEM((n_ch, 2, HALF), F32),
                pltpu.VMEM((2 * HALF, LANES), F32),
                pltpu.VMEM((HALF, LANES), F32),
                pltpu.VMEM((8, LANES), F32),
                pltpu.VMEM((group, 8, LANES), F32),
                pltpu.VMEM((8, LANES), F32),
                pltpu.VMEM((n_y, 8, LANES), F32),
                pltpu.VMEM((CHANS, ROWS), BF16),
                dma((12,)),
                dma((2,)),
                dma((n_ch,)),
                dma((n_ch,)),
                dma((group,)),
                dma((group,)),
                dma((n_y,)),
                dma((n_y,)),
                dma,
                pltpu.SemaphoreType.REGULAR,
                pltpu.VMEM((2, HALF), F32),
                pltpu.VMEM((n_ch, 2, HALF), F32),
                pltpu.VMEM((1, TAPS), F32),
                pltpu.VMEM((2 * n_ch, 1, TAPS), F32),
                pltpu.VMEM((CHANS, LANES), BF16),
                pltpu.VMEM((2, CHANS, LANES), BF16),
                pltpu.VMEM((8, LANES), F32),
                pltpu.VMEM((2, 8, LANES), F32),
                dma((n_ch,)),
                dma((n_ch,)),
                dma((2 * n_ch,)),
                dma((2 * n_ch,)),
                dma((4,)),
                dma((4,)),
            ],
            compiler_params=pltpu.CompilerParams(collective_id=0, has_side_effects=True),
            name="hyena_pair",
        )(
            q_mr,
            k_mr,
            v_mr,
            taps.T,
            gain.reshape(1, CHANS),
            q_li,
            k_li,
            rates.T,
            residues.T,
            skip.reshape(1, CHANS),
        )

    placed = (
        P("ch", "ctx"),
        P("ch", "ctx"),
        P("ch", "ctx"),
        P(None, "ch"),
        P("ch"),
        P("ch", "ctx"),
        P("ch", "ctx"),
        P("ch", None),
        P("ch", None),
        P("ch"),
    )
    return jax.shard_map(
        per_device, mesh=mesh, in_specs=placed, out_specs=P("ch", "ctx"), check_vma=False
    )


def solution(mesh):
    return build(mesh, 8)
```

```python
import functools

import jax
import jax.numpy as jnp
from jax import lax
from jax.experimental import pallas as pl
from jax.experimental.pallas import tpu as pltpu
from jax.sharding import PartitionSpec as P

MESH = pl.DeviceIdType.MESH
F32 = jnp.float32
BF16 = jnp.bfloat16

CHANS = 64
ROWS = 512
HALF = 256
TAPS = 128
MODES = 16
LANES = 128


def packed(block):
    block = block.astype(F32)
    return jnp.concatenate([block[:, :HALF], block[:, HALF:]], axis=0).T


def kernel(
    group,
    q_mr,
    k_mr,
    v_mr,
    taps,
    gain,
    q_li,
    k_li,
    rates,
    residues,
    skip,
    out,
    in5,
    taps_in,
    gain_in,
    rates_in,
    residues_in,
    skip_in,
    tails,
    a_own,
    rim,
    xs,
    far,
    tap_rows,
    wide,
    rate_rows,
    weight_rows,
    lift,
    filt,
    decay8,
    tail8,
    mr,
    sums_own,
    sums,
    vs,
    inner,
    state_own,
    states_z,
    total_own,
    states_y,
    result,
    in_sem,
    rim_sem,
    sums_send,
    sums_recv,
    z_send,
    z_recv,
    y_send,
    y_recv,
    out_sem,
    far_ready,
    early_own,
    early,
    first_own,
    first,
    raised_own,
    raised_in,
    main_own,
    main_in,
    early_send,
    early_recv,
    first_send,
    first_recv,
    raised_sem,
    main_sem,
):
    n_ctx, n_ch = lax.axis_size("ctx"), lax.axis_size("ch")
    n_y = n_ctx // group
    ctx, ch = lax.axis_index("ctx"), lax.axis_index("ch")
    place, plane = lax.rem(ctx, group), lax.div(ctx, group)
    core = lax.rem(ctx, 2)
    n_z = group // 2
    z = lax.div(place, 2)

    def at(dz, dcore):
        return 2 * lax.rem(z + dz, n_z) + lax.rem(core + dcore, 2)

    others = [(dz, dc) for dz in range(n_z) for dc in (0, 1) if (dz, dc) != (0, 0)]
    others = others[1:] + others[:1]

    hasty = (z >= 2) & (core == 0) if n_z == 4 else None
    late = z - 2

    def column_sums(gated):
        squares = (gated * gated).T
        return jnp.concatenate(
            [
                jnp.sum(squares[:CHANS], axis=0, keepdims=True),
                jnp.sum(squares[CHANS:], axis=0, keepdims=True),
            ],
            axis=0,
        )

    def send_early(peer, slot):
        return pltpu.make_async_remote_copy(
            src_ref=early_own,
            dst_ref=early.at[slot],
            send_sem=early_send.at[peer],
            recv_sem=early_recv.at[slot],
            device_id={"ctx": ctx, "ch": peer},
            device_id_type=MESH,
        )

    def send_first(dcore, peer, slot):
        return pltpu.make_async_remote_copy(
            src_ref=first_own,
            dst_ref=first.at[slot],
            send_sem=first_send.at[dcore * n_ch + peer],
            recv_sem=first_recv.at[slot],
            device_id={"ctx": plane * group + dcore, "ch": peer},
            device_id_type=MESH,
        )

    def send_plain(src, dst, sem, dcore, slot):
        return pltpu.make_async_remote_copy(
            src_ref=src,
            dst_ref=dst.at[slot],
            send_sem=sem.at[dcore],
            recv_sem=sem.at[2 + slot],
            device_id={"ctx": plane * group + dcore, "ch": ch},
            device_id_type=MESH,
        )

    rim[...] = jnp.zeros_like(rim)
    states_y[...] = jnp.zeros_like(states_y)

    barrier = pltpu.get_barrier_semaphore()

    def greet(device):
        pl.semaphore_signal(barrier, inc=1, device_id=device, device_id_type=MESH)

    def in_group(dz, dcore):
        return {"ctx": plane * group + at(dz, dcore), "ch": ch}

    @pl.when((place == 0) & (plane > 0))
    def _():
        greet({"ctx": ctx - 1, "ch": ch})

    @pl.when(z > 0)
    def _():
        for dc in (1, 0):
            greet(in_group(n_z - 1, dc))

    @pl.when(z < n_z - 1)
    def _():
        for dc in (0, 1):
            greet(in_group(1, dc))

    if n_z == 4:

        @pl.when(z == 0)
        def _():
            for place_late in (6, 4):
                for k in range(n_ch):
                    greet({"ctx": plane * group + place_late, "ch": lax.rem(ch + k, n_ch)})

    greet(in_group(0, 1))
    for k in range(1, n_ch):
        greet({"ctx": ctx, "ch": lax.rem(ch + k, n_ch)})
    for k in range(1, n_y):
        greet({"ctx": lax.rem(plane + k, n_y) * group + place, "ch": ch})

    tail = pl.ds(ROWS - TAPS, TAPS)
    loads = [
        pltpu.make_async_copy(src, dst, in_sem.at[i])
        for i, (src, dst) in enumerate(
            [
                (k_mr.at[:, tail], tails.at[0]),
                (v_mr.at[:, tail], tails.at[1]),
                (k_mr, in5.at[0]),
                (v_mr, in5.at[1]),
                (taps, taps_in),
                (rates, rates_in),
                (residues, residues_in),
                (q_mr, in5.at[2]),
                (k_li, in5.at[3]),
                (q_li, in5.at[4]),
                (gain, gain_in),
                (skip, skip_in),
            ]
        )
    ]
    for load in loads:
        load.start()

    lane = lax.broadcasted_iota(jnp.int32, (1, LANES), 1)
    first_half = lane < CHANS

    loads[0].wait()
    loads[1].wait()
    a_own[...] = (tails[0].astype(F32) * tails[1].astype(F32)).astype(BF16)
    loads[2].wait()
    loads[3].wait()
    a = (in5[0].astype(F32) * in5[1].astype(F32)).astype(BF16)
    a_t = packed(a)
    xs[TAPS:, :] = a_t
    xs[:TAPS, :] = jnp.where(first_half, 0.0, pltpu.roll(a_t[HALF - TAPS :], CHANS, 1))
    far[TAPS:, :] = jnp.zeros((CHANS, LANES), F32)

    for load in loads[4:]:
        load.wait()
    tap_half = taps_in[...].astype(F32)
    tap_rows[...] = jnp.concatenate([tap_half, tap_half], axis=0).T

    def doubled(ref):
        wide[...] = jnp.zeros_like(wide)
        wide[:, :CHANS] = ref[...]
        return wide[...] + pltpu.roll(wide[...], CHANS, 1)

    rate = doubled(rates_in)
    weight = doubled(residues_in) * jnp.sqrt(rate)
    rate_rows[...] = rate
    weight_rows[...] = weight

    def doubled_row(ref):
        wide[...] = jnp.zeros_like(wide)
        wide[:1, :CHANS] = ref[...]
        return (wide[...] + pltpu.roll(wide[...], CHANS, 1))[:1]

    gain_row = doubled_row(gain_in)
    skip_row = doubled_row(skip_in)

    q_t = packed(in5[2])
    k_t = packed(in5[3])

    def tap_step(i, acc):
        base = TAPS - 8 * i
        for p in range(8):
            acc = acc + xs[pl.ds(base - p, HALF), :] * tap_rows[pl.ds(8 * i + p, 1), :]
        return acc

    def own_taps():
        mr[...] = lax.fori_loop(0, TAPS // 8, tap_step, jnp.zeros((HALF, LANES), F32))

    if n_z == 4:
        pl.when(hasty)(own_taps)

    greeted = n_ch - 1 + n_y - 1 + 1
    greeted += jnp.where(z > 0, 2, 0) + jnp.where(z < n_z - 1, 2, 0)
    greeted += jnp.where((place == group - 1) & (plane < n_y - 1), 1, 0)
    if n_z == 4:
        greeted += jnp.where(hasty, 2 * n_ch, 0)
    pl.semaphore_wait(barrier, greeted)

    def send_rim():
        return pltpu.make_async_remote_copy(
            src_ref=a_own,
            dst_ref=rim,
            send_sem=rim_sem.at[0],
            recv_sem=rim_sem.at[1],
            device_id={"ctx": ctx + 1, "ch": ch},
            device_id_type=MESH,
        )

    @pl.when(ctx < n_ctx - 1)
    def _():
        send_rim().start()

    def tell(sem, dz, dcore):
        pl.semaphore_signal(sem, inc=1, device_id=in_group(dz, dcore), device_id_type=MESH)

    if n_z == 4:

        @pl.when(z == 1)
        def _():
            tell(far_ready, 1, 0)

        @pl.when(z == 2)
        def _():
            tell(far_ready, n_z - 1, 0)

        @pl.when(hasty)
        def _():
            gated = q_t * mr[...]
            mine = column_sums(gated)
            early_own[...] = mine
            early[ch] = mine
            for k in range(1, n_ch):
                send_early(lax.rem(ch + k, n_ch), ch).start()

    if n_z == 4:
        pl.when(jnp.logical_not(hasty))(own_taps)
    else:
        own_taps()

    @pl.when(ctx > 0)
    def _():
        send_rim().wait_recv()

    rim_now = rim[...].astype(F32)
    later = jnp.where(first_half, pltpu.roll(rim_now, CHANS, 1), 0.0)
    far[:TAPS, :] = jnp.concatenate([rim_now, later], axis=0).T

    def far_step(i, acc):
        base = TAPS - 8 * i
        for p in range(8):
            acc = acc + far[pl.ds(base - p, CHANS), :] * tap_rows[pl.ds(8 * i + p, 1), :]
        return acc

    reach = lax.fori_loop(0, TAPS // 8, far_step, jnp.zeros((CHANS, LANES), F32))
    mr[:CHANS, :] += jnp.where(first_half, reach, 0.0)
    mr[CHANS:TAPS, :] += jnp.where(first_half, pltpu.roll(reach, CHANS, 1), 0.0)

    gated = q_t * mr[...]
    mine = column_sums(gated)
    sums_own[...] = mine
    sums[ch] = mine

    def send_sums(peer, slot):
        return pltpu.make_async_remote_copy(
            src_ref=sums_own,
            dst_ref=sums.at[slot],
            send_sem=sums_send.at[peer],
            recv_sem=sums_recv.at[slot],
            device_id={"ctx": ctx, "ch": peer},
            device_id_type=MESH,
        )

    raised = k_t * gated

    if n_z == 4:

        @pl.when(hasty)
        def _():
            first_own[...] = mine[:1, :TAPS]
            for dcore in (0, 1):
                for k in range(n_ch):
                    send_first(dcore, lax.rem(ch + k, n_ch), late * n_ch + ch).start()
            raised_own[...] = jnp.where(
                first_half, raised[:CHANS], pltpu.roll(raised[CHANS:TAPS], CHANS, 1)
            ).astype(BF16)
            for dcore in (0, 1):
                send_plain(raised_own, raised_in, raised_sem, dcore, late).start()

    for k in range(1, n_ch):
        send_sums(lax.rem(ch + k, n_ch), ch).start()

    if n_z == 4:

        @pl.when(z == 1)
        def _():
            pl.semaphore_wait(far_ready, 1)
            tell(far_ready, n_z - 1, 0)

        @pl.when(z == 2)
        def _():
            pl.semaphore_wait(far_ready, 1)
            tell(far_ready, 1, 0)

    times = lax.broadcasted_iota(jnp.int32, (HALF, LANES), 0).astype(F32)
    filt[...] = jnp.zeros_like(filt)

    @pl.loop(0, MODES)
    def _(r):
        term = jnp.exp(-rate_rows[pl.ds(r, 1), :] * times) * weight_rows[pl.ds(r, 1), :]
        lift[r] = term
        filt[...] += term

    offset8 = lax.broadcasted_iota(jnp.int32, (1, 8, LANES), 1).astype(F32)
    decay8[...] = jnp.broadcast_to(jnp.exp(rate * -8.0)[:, None, :], (MODES, 8, LANES))
    tail8[...] = jnp.exp(-rate[:, None, :] * (7.0 - offset8))

    def normed(sums):
        total = sums[0]
        for k in range(1, n_ch):
            total = total + sums[k]
        inv = lax.rsqrt(total / (n_ch * CHANS) + 1e-05)
        inv_t = jnp.concatenate(
            [
                jnp.broadcast_to(inv[:1], (CHANS, HALF)),
                jnp.broadcast_to(inv[1:], (CHANS, HALF)),
            ],
            axis=0,
        ).T
        return (raised * inv_t * gain_row).astype(BF16).astype(F32)

    def ends_of(v):
        keep = decay8[...]
        acc = jnp.broadcast_to(v[None, :8], (MODES, 8, LANES))
        for i in range(1, v.shape[0] // 8):
            acc = acc * keep + v[None, 8 * i : 8 * i + 8]
        return jnp.sum(acc * tail8[...], axis=1)

    def folded(x):
        return jnp.where(first_half, x[:8], x[8:])

    def joined(aged):
        return folded(aged + pltpu.roll(aged, CHANS, 1))

    decay_half = jnp.exp(rate * -float(HALF))

    if n_z == 4:

        @pl.when(hasty)
        def _():
            for k in range(1, n_ch):
                peer = lax.rem(ch + k, n_ch)
                send_early(peer, peer).wait_recv()
            row = lax.broadcasted_iota(jnp.int32, (HALF, LANES), 0)
            v = jnp.where(first_half & (row < TAPS), 0.0, normed(early))
            ends = ends_of(v)
            main_own[...] = joined(jnp.where(first_half, ends * decay_half, ends))
            for dcore in (0, 1):
                send_plain(main_own, main_in, main_sem, dcore, late).start()

    for k in range(1, n_ch):
        peer = lax.rem(ch + k, n_ch)
        send_sums(peer, peer).wait_recv()

    v = normed(sums)
    vs[:HALF, :] = jnp.zeros((HALF, LANES), F32)
    vs[HALF:, :] = v

    ends_half = ends_of(v)
    state = joined(jnp.where(first_half, ends_half * decay_half, ends_half))
    from_first = pltpu.roll(ends_half, CHANS, 1)
    state_own[...] = state
    states_z[place] = state

    def send_z(peer, slot):
        return pltpu.make_async_remote_copy(
            src_ref=state_own,
            dst_ref=states_z.at[slot],
            send_sem=z_send.at[peer],
            recv_sem=z_recv.at[slot],
            device_id={"ctx": plane * group + peer, "ch": ch},
            device_id_type=MESH,
        )

    if n_z == 4:

        @pl.when((z == 0) | (z == n_z - 1))
        def _():
            pl.semaphore_wait(far_ready, 1)

    def for_others(act, sending):
        for step in others:
            peer = at(*step)
            if n_z == 4 and step[0] > 0:
                replaced = (
                    hasty & (peer < 2) if sending else (z == 0) & (peer >= 4) & (lax.rem(peer, 2) == 0)
                )

                @pl.when(jnp.logical_not(replaced))
                def _(peer=peer):
                    act(send_z(peer, place if sending else peer))

            else:
                act(send_z(peer, place if sending else peer))

    for_others(lambda copy: copy.start(), True)

    def own_filter():
        inner[...] = skip_row * v
        block = 64
        for b in range(HALF // block):
            low = b * block

            def filt_step(i, acc, low=low):
                base = HALF - 8 * i
                for p in range(8):
                    acc = acc + vs[pl.ds(base - p, HALF - low), :] * filt[pl.ds(low + 8 * i + p, 1), :]
                return acc

            inner[low:, :] += lax.fori_loop(
                0, block // 8, filt_step, jnp.zeros((HALF - low, LANES), F32)
            )

    waited_for = (plane > 0) & (plane < n_y - 1)
    pl.when(jnp.logical_not(waited_for))(own_filter)
    rate_folded = folded(rate)
    decay_one = jnp.exp(rate_folded * -float(ROWS))
    decay_plane = jnp.exp(rate_folded * -float(ROWS * group))
    decay_place = jnp.exp(rate_folded * (place.astype(F32) * -float(ROWS)))

    if n_z == 4:

        @pl.when(z == 0)
        def _():
            for slot in (1, 0):
                for k in range(n_ch):
                    send_first(0, k, slot * n_ch + k).wait_recv()
                total = first[slot * n_ch]
                for k in range(1, n_ch):
                    total = total + first[slot * n_ch + k]
                inv = lax.rsqrt(total / (n_ch * CHANS) + 1e-05)
                inv_t = jnp.concatenate(
                    [
                        jnp.broadcast_to(inv, (CHANS, LANES)),
                        jnp.broadcast_to(pltpu.roll(inv, CHANS, 1), (CHANS, LANES)),
                    ],
                    axis=0,
                ).T[:CHANS]
                send_plain(raised_own, raised_in, raised_sem, 0, slot).wait_recv()
                v = (raised_in[slot].astype(F32) * inv_t * gain_row).astype(BF16).astype(F32)
                age = jnp.where(first_half, float(ROWS - CHANS), float(ROWS - TAPS))
                added = joined(ends_of(v) * jnp.exp(-rate * age))
                send_plain(main_own, main_in, main_sem, 0, slot).wait_recv()
                states_z[4 + 2 * slot] = main_in[slot] + added

    for_others(lambda copy: copy.wait_recv(), False)
    run = jnp.zeros((8, LANES), F32)
    before = jnp.zeros((8, LANES), F32)
    for k in range(group):
        before = jnp.where(place == k, run, before)
        run = run * decay_one + states_z[k]
    total_own[...] = run

    def send_y(peer, slot):
        return pltpu.make_async_remote_copy(
            src_ref=total_own,
            dst_ref=states_y.at[slot],
            send_sem=y_send.at[peer],
            recv_sem=y_recv.at[slot],
            device_id={"ctx": peer * group + place, "ch": ch},
            device_id_type=MESH,
        )

    for k in range(1, n_y):

        @pl.when(plane + k < n_y)
        def _(k=k):
            send_y(plane + k, plane).start()

    pl.when(waited_for)(own_filter)
    ql_t = packed(in5[4])
    for k in range(1, n_y):

        @pl.when(plane - k >= 0)
        def _(k=k):
            send_y(plane - k, plane - k).wait_recv()

    carry = jnp.zeros((8, LANES), F32)
    for k in range(n_y - 1):
        carry = jnp.where(plane > k, carry * decay_plane + states_y[k], carry)
    carry = before + decay_place * carry

    low = jnp.where(first_half, carry, 0.0)
    high = jnp.where(first_half, 0.0, carry)
    carry = jnp.concatenate(
        [low + pltpu.roll(low, CHANS, 1), high + pltpu.roll(high, CHANS, 1)], axis=0
    )
    carry = jnp.where(first_half, carry, carry * decay_half + from_first)
    carry = carry * jnp.exp(-rate)
    acc = inner[...]
    for r in range(MODES):
        acc = acc + lift[r] * carry[r : r + 1]
    mixed = (ql_t * acc.astype(BF16).astype(F32)).T.astype(BF16)
    result[:, :HALF] = mixed[:CHANS]
    result[:, HALF:] = mixed[CHANS:]
    out[...] = result[...]

    @pl.when(ctx < n_ctx - 1)
    def _():
        send_rim().wait_send()

    for k in range(1, n_ch):
        send_sums(lax.rem(ch + k, n_ch), ch).wait_send()
    for_others(lambda copy: copy.wait_send(), True)
    if n_z == 4:

        @pl.when(hasty)
        def _():
            for k in range(1, n_ch):
                send_early(lax.rem(ch + k, n_ch), ch).wait_send()
            for dcore in (0, 1):
                for k in range(n_ch):
                    send_first(dcore, lax.rem(ch + k, n_ch), late * n_ch + ch).wait_send()
                send_plain(raised_own, raised_in, raised_sem, dcore, late).wait_send()
                send_plain(main_own, main_in, main_sem, dcore, late).wait_send()

    for k in range(1, n_y):

        @pl.when(plane + k < n_y)
        def _(k=k):
            send_y(plane + k, plane).wait_send()


def build(mesh, group):
    n_ctx, n_ch = mesh.shape["ctx"], mesh.shape["ch"]
    n_y = n_ctx // group

    def per_device(q_mr, k_mr, v_mr, taps, gain, q_li, k_li, rates, residues, skip):
        dma = pltpu.SemaphoreType.DMA
        any_spec = pl.BlockSpec(memory_space=pl.ANY)
        return pl.pallas_call(
            functools.partial(kernel, group),
            out_shape=pltpu.VMEM((CHANS, ROWS), BF16),
            in_specs=[any_spec] * 10,
            out_specs=pl.BlockSpec(memory_space=pltpu.VMEM),
            scratch_shapes=[
                pltpu.VMEM((5, CHANS, ROWS), BF16),
                pltpu.VMEM((CHANS, TAPS), BF16),
                pltpu.VMEM((1, CHANS), F32),
                pltpu.VMEM((MODES, CHANS), F32),
                pltpu.VMEM((MODES, CHANS), F32),
                pltpu.VMEM((1, CHANS), F32),
                pltpu.VMEM((2, CHANS, TAPS), BF16),
                pltpu.VMEM((CHANS, TAPS), BF16),
                pltpu.VMEM((CHANS, TAPS), BF16),
                pltpu.VMEM((TAPS + HALF, LANES), F32),
                pltpu.VMEM((TAPS + CHANS, LANES), F32),
                pltpu.VMEM((TAPS, LANES), F32),
                pltpu.VMEM((MODES, LANES), F32),
                pltpu.VMEM((MODES, LANES), F32),
                pltpu.VMEM((MODES, LANES), F32),
                pltpu.VMEM((MODES, HALF, LANES), F32),
                pltpu.VMEM((HALF, LANES), F32),
                pltpu.VMEM((MODES, 8, LANES), F32),
                pltpu.VMEM((MODES, 8, LANES), F32),
                pltpu.VMEM((HALF, LANES), F32),
                pltpu.VMEM((2, HALF), F32),
                pltpu.VMEM((n_ch, 2, HALF), F32),
                pltpu.VMEM((2 * HALF, LANES), F32),
                pltpu.VMEM((HALF, LANES), F32),
                pltpu.VMEM((8, LANES), F32),
                pltpu.VMEM((group, 8, LANES), F32),
                pltpu.VMEM((8, LANES), F32),
                pltpu.VMEM((n_y, 8, LANES), F32),
                pltpu.VMEM((CHANS, ROWS), BF16),
                dma((12,)),
                dma((2,)),
                dma((n_ch,)),
                dma((n_ch,)),
                dma((group,)),
                dma((group,)),
                dma((n_y,)),
                dma((n_y,)),
                dma,
                pltpu.SemaphoreType.REGULAR,
                pltpu.VMEM((2, HALF), F32),
                pltpu.VMEM((n_ch, 2, HALF), F32),
                pltpu.VMEM((1, TAPS), F32),
                pltpu.VMEM((2 * n_ch, 1, TAPS), F32),
                pltpu.VMEM((CHANS, LANES), BF16),
                pltpu.VMEM((2, CHANS, LANES), BF16),
                pltpu.VMEM((8, LANES), F32),
                pltpu.VMEM((2, 8, LANES), F32),
                dma((n_ch,)),
                dma((n_ch,)),
                dma((2 * n_ch,)),
                dma((2 * n_ch,)),
                dma((4,)),
                dma((4,)),
            ],
            compiler_params=pltpu.CompilerParams(collective_id=0, has_side_effects=True),
            name="hyena_pair",
        )(
            q_mr,
            k_mr,
            v_mr,
            taps.T,
            gain.reshape(1, CHANS),
            q_li,
            k_li,
            rates.T,
            residues.T,
            skip.reshape(1, CHANS),
        )

    placed = (
        P("ch", "ctx"),
        P("ch", "ctx"),
        P("ch", "ctx"),
        P(None, "ch"),
        P("ch"),
        P("ch", "ctx"),
        P("ch", "ctx"),
        P("ch", None),
        P("ch", None),
        P("ch"),
    )
    return jax.shard_map(
        per_device, mesh=mesh, in_specs=placed, out_specs=P("ch", "ctx"), check_vma=False
    )


def solution(mesh):
    return build(mesh, 8)
```
